512 devices in a mesh: band: 8 (over x_lo, y), lon: 64 (over x_hi, z, core).
Axes of the slice: x: 4 (x_hi: 2, x_lo: 2; x = x_hi * 2 + x_lo), y: 4, z: 16, core: 2. Of those that a mesh axis runs over, the one named last changes fastest.
Arguments:
- tracers: float32 [384, 1024, 128], P('band', 'lon'), may hold values from -6 to 6
- lon_offset: int32 [384, 4], P('band'), may hold values from -512 to 511
- lon_weights: float32 [4, 384, 4], P(None, 'band'), may hold values from -0.1 to 1, as said below
- lat_offset: int32 [384, 4], P('band'), may hold values from -6 to 6
- lat_weights: float32 [4, 384, 4], P(None, 'band'), may hold values from -0.1 to 1, as said below
Outputs:
- advected: float32 [384, 1024, 128], P('band', 'lon')
The draws below stay inside these ranges and needn't reach their ends.
Inputs may be any that keep to these rules, and one draw needn't show every extreme that they name: `lon_weights`: each set of four weights sums to one. `lat_weights`: each set of four weights sums to one.
All inputs are finite; a program needn't handle non-finite values.
Results may differ from the reference program's by a relative error of at most 0.0003.
Values sent between devices are 32-bit elements; how exact they have to be, the bound alone decides.
No kernel may reach another device: no remote copies, remote signals or barrier semaphores. Data moves between devices by JAX's collectives and lax.ppermute only.
A program may use at most 64 MiB of HBM per device.

```python
import jax
import jax.numpy as jnp
from jax import lax

LEV = 4
TRACERS = 32
TMAX = 6
NLAT = 384
NLON = 1024
COLS = 128


def cubic_table(key):
    frac = jax.random.uniform(key, (NLAT, LEV), jnp.float32)
    left = -frac * (1.0 - frac) * (2.0 - frac) / 6.0
    centre = (1.0 + frac) * (1.0 - frac) * (2.0 - frac) / 2.0
    right = (1.0 + frac) * frac * (2.0 - frac) / 2.0
    outer = -(1.0 + frac) * frac * (1.0 - frac) / 6.0
    return jnp.stack([left, centre, right, outer]).astype(jnp.float32)


def draw_lon_weights(key, part):
    return cubic_table(jax.random.fold_in(key, 11))


def draw_lat_weights(key, part):
    return cubic_table(jax.random.fold_in(key, 12))


def draw_lon_offset(key, part):
    rows = jnp.arange(NLAT, dtype=jnp.int32)
    dist = jnp.abs(2 * rows - (NLAT - 1))
    reach = 2 + (NLON // 2 - 2) * dist * dist // ((NLAT - 1) * (NLAT - 1))
    values = jax.random.randint(jax.random.fold_in(key, 13), (NLAT, LEV), -reach[:, None], reach[:, None] + 1, dtype=jnp.int32)
    values = jnp.minimum(values, NLON // 2 - 1)
    values = values.at[0, 0].set(NLON // 2 - 1)
    values = values.at[NLAT - 1, 0].set(-(NLON // 2))
    return values


def with_ends(entries, rng, smallest, high):
    index_at = [jax.random.randint(jax.random.fold_in(rng, axis), (), 0, length) for axis, length in enumerate(entries.shape)]
    main_axis = entries.shape.index(max(entries.shape))
    beside = index_at[:main_axis] + [(index_at[main_axis] + 1) % entries.shape[main_axis]] + index_at[main_axis + 1:]
    return entries.at[tuple(index_at)].set(smallest).at[tuple(beside)].set(high)


def steps_of(own_key, shape, cuts, least, high):
    factor_of, own = 1.0, jax.random.fold_in(own_key, 6)
    for dim, shards_of in cuts:
        steps = jnp.exp(jax.random.uniform(jax.random.fold_in(own, dim), (shards_of,), jnp.float32, least / len(cuts), high / len(cuts)))
        factor_of = factor_of * jnp.repeat(steps, shape[dim] // shards_of).reshape([-1 if axis == dim else 1 for axis in range(len(shape))])
    return factor_of


def bell_draw(key, extent, width, most, cuts=(), kind=jnp.bfloat16):
    array = jax.random.normal(key, extent, jnp.float32) * width
    if len(cuts) > 0:
        array = steps_of(key, extent, cuts, -0.22, 0.18) * array
    return jnp.clip(array, min=-most, max=most).astype(kind)


def setup_inputs(seed: int = 0) -> dict:
    streams_of = jax.random.split(jax.random.key(seed), 6)
    return {
        "tracers": bell_draw(streams_of[0], (NLAT, NLON, COLS), 1.0, 6.0, ((0, 8), (1, 64)), jnp.float32),
        "lon_offset": draw_lon_offset(jax.random.fold_in(streams_of[5], 71), 0),
        "lon_weights": draw_lon_weights(jax.random.fold_in(streams_of[5], 71), 0),
        "lat_offset": with_ends(jax.random.randint(streams_of[3], (NLAT, LEV), -TMAX, TMAX + 1), jax.random.fold_in(streams_of[3], 1), -TMAX, TMAX).astype(jnp.int32),
        "lat_weights": draw_lat_weights(jax.random.fold_in(streams_of[5], 71), 0),
    }


def zonal_pass(field, offsets, weights):
    cells = jnp.arange(NLON, dtype=jnp.int32)
    rows = jnp.arange(NLAT, dtype=jnp.int32)

    def one_level(packed):
        plane, shifts, coeffs = packed
        total = jnp.zeros_like(plane)
        for k in range(4):
            index = jnp.mod(cells[None, :] - shifts[:, None] + (k - 1), NLON).astype(jnp.int32)
            total = total + coeffs[k][:, None, None] * plane[rows[:, None], index]
        return total

    result = lax.map(one_level, (field.transpose(2, 0, 1, 3), offsets.T, weights.transpose(2, 0, 1)))
    return result.transpose(1, 2, 0, 3)


def meridional_pass(field, offsets, weights):
    rows = jnp.arange(NLAT, dtype=jnp.int32)

    def one_level(packed):
        plane, shifts, coeffs = packed
        total = jnp.zeros_like(plane)
        for k in range(4):
            source = jnp.clip(rows - shifts + (k - 1), 0, NLAT - 1).astype(jnp.int32)
            total = total + coeffs[k][:, None, None] * plane[source]
        return total

    result = lax.map(one_level, (field.transpose(2, 0, 1, 3), offsets.T, weights.transpose(2, 0, 1)))
    return result.transpose(1, 2, 0, 3)


def reference(tracers, lon_offset, lon_weights, lat_offset, lat_weights):
    field = tracers.reshape(NLAT, NLON, LEV, TRACERS)
    first = zonal_pass(field, lon_offset, lon_weights)
    second = meridional_pass(first, lat_offset, lat_weights)
    third = zonal_pass(second, lon_offset, lon_weights)
    return third.reshape(NLAT, NLON, LEV * TRACERS)
```

```python
import functools

import jax
import jax.numpy as jnp
from jax import lax
from jax.experimental import pallas as pl
from jax.experimental.pallas import tpu as pltpu
from jax.sharding import PartitionSpec as P

TMAX = 6
REACH = 8
VMEM = pltpu.VMEM
SMEM = pltpu.SMEM


def turn_kernel(x_ref, o_ref):
    for i in range(x_ref.shape[0] // 128):
        for j in range(x_ref.shape[1] // 128):
            o_ref[j * 128 : (j + 1) * 128, i * 128 : (i + 1) * 128] = x_ref[
                i * 128 : (i + 1) * 128, j * 128 : (j + 1) * 128
            ].T


def turned(x):
    return pl.pallas_call(
        turn_kernel,
        out_shape=jax.ShapeDtypeStruct((x.shape[1], x.shape[0]), x.dtype),
        in_specs=[pl.BlockSpec(memory_space=VMEM)],
        out_specs=pl.BlockSpec(memory_space=VMEM),
        name="turn",
    )(x)


def rotate(line, offset, weights, ext_ref, cells, lanes_per_block):
    lanes = line.shape[1]
    circle = lanes // lanes_per_block * cells
    wrapped = lax.rem(offset + circle, circle)
    step = lax.div(wrapped, cells) * lanes_per_block
    rest = lax.rem(wrapped, cells)
    before = lax.rem(step + lanes_per_block, lanes)
    after = lax.rem(step + lanes - lanes_per_block, lanes)
    ext_ref[0:cells] = pltpu.roll(line, before, 1)
    ext_ref[cells : 2 * cells] = pltpu.roll(line, step, 1)
    ext_ref[2 * cells : 2 * cells + 8] = pltpu.roll(line[0:8], after, 1)
    total = None
    for k in range(4):
        term = weights[k] * ext_ref[pl.ds(cells - 1 - rest + k, cells), :]
        total = term if total is None else total + term
    return total


def first_kernel(cells, per_block, levels, x_ref, off_ref, w_ref, o_ref, turn_ref, ext_ref):
    rows = x_ref.shape[1] // cells
    level = lax.div(lax.axis_index("lon") * levels, lax.axis_size("lon"))
    for i in range(x_ref.shape[1] // 128):
        turn_ref[i * 128 : (i + 1) * 128, :] = x_ref[:, i * 128 : (i + 1) * 128].T
    for r in range(rows):
        weights = [w_ref[k, r, level] for k in range(4)]
        o_ref[r * cells : (r + 1) * cells, :] = rotate(
            turn_ref[r * cells : (r + 1) * cells, :],
            off_ref[r, level],
            weights,
            ext_ref.at[r],
            cells,
            per_block,
        )


def second_kernel(
    cells, per_block, levels, f_ref, lo_ref, hi_ref, off_ref, w_ref, toff_ref, tw_ref, o_ref, all_ref, turn_ref, ext_ref
):
    rows = f_ref.shape[0] // cells
    level = lax.div(lax.axis_index("lon") * levels, lax.axis_size("lon"))
    first_row = lax.axis_index("band") * rows
    last_row = lax.axis_size("band") * rows - 1
    edge = REACH * cells
    all_ref[0:edge] = lo_ref[...]
    all_ref[edge : edge + rows * cells] = f_ref[...]
    all_ref[edge + rows * cells : 2 * edge + rows * cells] = hi_ref[...]
    for r in range(rows):
        shift = toff_ref[r, level]
        total = None
        for k in range(4):
            source = jnp.clip(first_row + r - shift + (k - 1), 0, last_row) - first_row + REACH
            term = tw_ref[k, r, level] * all_ref[pl.ds(pl.multiple_of(source * cells, cells), cells), :]
            total = term if total is None else total + term
        weights = [w_ref[k, r, level] for k in range(4)]
        turn_ref[r * cells : (r + 1) * cells, :] = rotate(
            total, off_ref[r, level], weights, ext_ref.at[r], cells, per_block
        )
    for i in range(o_ref.shape[1] // 128):
        o_ref[:, i * 128 : (i + 1) * 128] = turn_ref[i * 128 : (i + 1) * 128, :].T


def spread(x, groups):
    n, m = x.shape
    y = lax.all_to_all(x.reshape(groups, n // groups, m), "lon", 0, 0, tiled=True)
    return y.reshape(n, m)


def per_device(tracers, lon_offset, lon_weights, lat_offset, lat_weights):
    rows, cells, columns = tracers.shape
    levels = lon_offset.shape[1]
    groups = lax.axis_size("lon")
    per_block = columns // groups
    bands = lax.axis_size("band")
    flat = rows * cells
    edge = REACH * cells
    vspec = pl.BlockSpec(memory_space=VMEM)
    sspec = pl.BlockSpec(memory_space=SMEM)

    gathered = spread(turned(tracers.reshape(flat, columns)), groups)
    first = pl.pallas_call(
        functools.partial(first_kernel, cells, per_block, levels),
        out_shape=jax.ShapeDtypeStruct((flat, columns), jnp.float32),
        in_specs=[vspec, sspec, sspec],
        out_specs=vspec,
        scratch_shapes=[VMEM((flat, columns), jnp.float32), VMEM((rows, 2 * cells + 8, columns), jnp.float32)],
        name="first",
    )(gathered, lon_offset, lon_weights)
    lo = lax.ppermute(first[flat - edge :], "band", [(i, i + 1) for i in range(bands - 1)])
    hi = lax.ppermute(first[:edge], "band", [(i + 1, i) for i in range(bands - 1)])
    out = pl.pallas_call(
        functools.partial(second_kernel, cells, per_block, levels),
        out_shape=jax.ShapeDtypeStruct((columns, flat), jnp.float32),
        in_specs=[vspec, vspec, vspec, sspec, sspec, sspec, sspec],
        out_specs=vspec,
        scratch_shapes=[
            VMEM((flat + 2 * edge, columns), jnp.float32),
            VMEM((flat, columns), jnp.float32),
            VMEM((rows, 2 * cells + 8, columns), jnp.float32),
        ],
        name="second",
    )(first, lo, hi, lon_offset, lon_weights, lat_offset, lat_weights)
    return turned(spread(out, groups)).reshape(rows, cells, columns)


def solution(mesh):
    return jax.shard_map(
        per_device,
        mesh=mesh,
        in_specs=(
            P("band", "lon", None),
            P("band", None),
            P(None, "band", None),
            P("band", None),
            P(None, "band", None),
        ),
        out_specs=P("band", "lon", None),
        check_vma=False,
    )
```

```python
import functools

import jax
import jax.numpy as jnp
from jax import lax
from jax.experimental import pallas as pl
from jax.experimental.pallas import tpu as pltpu
from jax.sharding import PartitionSpec as P

TMAX = 6
REACH = 8
VMEM = pltpu.VMEM
SMEM = pltpu.SMEM
PARAMS = pltpu.CompilerParams(vmem_limit_bytes=8 * 1024 * 1024)


def turn_kernel(x_ref, o_ref):
    for i in range(x_ref.shape[0] // 128):
        for j in range(x_ref.shape[1] // 128):
            o_ref[j * 128 : (j + 1) * 128, i * 128 : (i + 1) * 128] = x_ref[
                i * 128 : (i + 1) * 128, j * 128 : (j + 1) * 128
            ].T


def turned(x):
    return pl.pallas_call(
        turn_kernel,
        out_shape=jax.ShapeDtypeStruct((x.shape[1], x.shape[0]), x.dtype),
        in_specs=[pl.BlockSpec(memory_space=VMEM)],
        out_specs=pl.BlockSpec(memory_space=VMEM),
        compiler_params=PARAMS,
        name="turn",
    )(x)


def rotate(line, offset, weights, ext_ref, cells, lanes_per_block):
    lanes = line.shape[1]
    circle = lanes // lanes_per_block * cells
    wrapped = offset & (circle - 1)
    rest = wrapped & (cells - 1)
    step = (wrapped >> (cells.bit_length() - 1)) * lanes_per_block
    before = (step + lanes_per_block) & (lanes - 1)
    after = (step + lanes - lanes_per_block) & (lanes - 1)
    ext_ref[0:cells] = pltpu.roll(line, before, 1)
    ext_ref[cells : 2 * cells] = pltpu.roll(line, step, 1)
    ext_ref[2 * cells : 2 * cells + 8] = pltpu.roll(line[0:8], after, 1)
    total = None
    for k in range(4):
        term = weights[k] * ext_ref[pl.ds(cells - 1 - rest + k, cells), :]
        total = term if total is None else total + term
    return total


def first_kernel(cells, per_block, levels, x_ref, off_ref, w_ref, o_ref, head_ref, tail_ref, turn_ref, ext_ref):
    rows = x_ref.shape[1] // cells
    level = lax.div(lax.axis_index("lon") * levels, lax.axis_size("lon"))
    for i in range(x_ref.shape[1] // 128):
        turn_ref[i * 128 : (i + 1) * 128, :] = x_ref[:, i * 128 : (i + 1) * 128].T
    for r in range(rows):
        value = rotate(
            turn_ref[r * cells : (r + 1) * cells, :],
            off_ref[level, r],
            [w_ref[k, level, r] for k in range(4)],
            ext_ref.at[r],
            cells,
            per_block,
        )
        o_ref[r * cells : (r + 1) * cells, :] = value
        if r < REACH:
            head_ref[r * cells : (r + 1) * cells, :] = value
        if r >= rows - REACH:
            s = r - (rows - REACH)
            tail_ref[s * cells : (s + 1) * cells, :] = value


def rows_done(chosen, rows, cells, per_block, levels, source_ref, first_place, scalars, o_ref, turn_ref, ext_ref):
    off_ref, w_ref, toff_ref, tw_ref = scalars
    level = lax.div(lax.axis_index("lon") * levels, lax.axis_size("lon"))
    first_row = lax.axis_index("band") * rows
    last_row = lax.axis_size("band") * rows - 1
    for r in chosen:
        shift = toff_ref[level, r]
        total = None
        for k in range(4):
            source = jnp.clip(first_row + (r + k - 1) - shift, 0, last_row) - first_row - first_place
            term = tw_ref[k, level, r] * source_ref[pl.ds(pl.multiple_of(source * cells, cells), cells), :]
            total = term if total is None else total + term
        turn_ref[r * cells : (r + 1) * cells, :] = rotate(
            total, off_ref[level, r], [w_ref[k, level, r] for k in range(4)], ext_ref.at[r], cells, per_block
        )
    per_turn = 128 // cells
    for i in sorted({r // per_turn for r in chosen}):
        o_ref[:, i * 128 : (i + 1) * 128] = turn_ref[i * 128 : (i + 1) * 128, :].T


def inner_kernel(cells, per_block, levels, f_ref, off_ref, w_ref, toff_ref, tw_ref, o_ref, turn_ref, ext_ref):
    rows = f_ref.shape[0] // cells
    scalars = (off_ref, w_ref, toff_ref, tw_ref)
    chosen = range(REACH, rows - REACH)
    rows_done(chosen, rows, cells, per_block, levels, f_ref, 0, scalars, o_ref, turn_ref, ext_ref)


def outer_kernel(
    cells, per_block, levels, f_ref, lo_ref, hi_ref, off_ref, w_ref, toff_ref, tw_ref, i_ref, o_ref, all_ref, turn_ref, ext_ref
):
    rows = f_ref.shape[0] // cells
    edge = REACH * cells
    flat = rows * cells
    scalars = (off_ref, w_ref, toff_ref, tw_ref)
    all_ref[0:edge] = lo_ref[...]
    all_ref[edge : 3 * edge] = f_ref[0 : 2 * edge]
    all_ref[flat - edge : flat + edge] = f_ref[flat - 2 * edge :]
    all_ref[flat + edge : flat + 2 * edge] = hi_ref[...]
    chosen = [*range(REACH), *range(rows - REACH, rows)]
    rows_done(chosen, rows, cells, per_block, levels, all_ref, -REACH, scalars, o_ref, turn_ref, ext_ref)


def spread(x, groups):
    n, m = x.shape
    y = lax.all_to_all(x.reshape(groups, n // groups, m), "lon", 0, 0, tiled=True)
    return y.reshape(n, m)


def per_device(tracers, lon_offset, lon_weights, lat_offset, lat_weights):
    rows, cells, columns = tracers.shape
    levels = lon_offset.shape[1]
    groups = lax.axis_size("lon")
    per_block = columns // groups
    bands = lax.axis_size("band")
    flat = rows * cells
    edge = REACH * cells
    f32 = jnp.float32
    vspec = pl.BlockSpec(memory_space=VMEM)
    sspec = pl.BlockSpec(memory_space=SMEM)
    scalars = (lon_offset.T, lon_weights.transpose(0, 2, 1), lat_offset.T, lat_weights.transpose(0, 2, 1))
    scratch = [VMEM((flat, columns), f32), VMEM((rows, 2 * cells + 8, columns), f32)]

    gathered = spread(turned(tracers.reshape(flat, columns)), groups)
    first, head, tail = pl.pallas_call(
        functools.partial(first_kernel, cells, per_block, levels),
        out_shape=[jax.ShapeDtypeStruct((n, columns), f32) for n in (flat, edge, edge)],
        in_specs=[vspec, sspec, sspec],
        out_specs=[vspec] * 3,
        scratch_shapes=scratch,
        compiler_params=PARAMS,
        name="first",
    )(gathered, *scalars[:2])
    lo = lax.ppermute(tail, "band", [(i, i + 1) for i in range(bands - 1)])
    hi = lax.ppermute(head, "band", [(i + 1, i) for i in range(bands - 1)])
    inner = pl.pallas_call(
        functools.partial(inner_kernel, cells, per_block, levels),
        out_shape=jax.ShapeDtypeStruct((columns, flat), f32),
        in_specs=[vspec] + [sspec] * 4,
        out_specs=vspec,
        scratch_shapes=scratch,
        compiler_params=PARAMS,
        name="inner",
    )(first, *scalars)
    out = pl.pallas_call(
        functools.partial(outer_kernel, cells, per_block, levels),
        out_shape=jax.ShapeDtypeStruct((columns, flat), f32),
        in_specs=[vspec] * 3 + [sspec] * 4 + [vspec],
        out_specs=vspec,
        scratch_shapes=[VMEM((flat + 2 * edge, columns), f32), *scratch],
        input_output_aliases={7: 0},
        compiler_params=PARAMS,
        name="outer",
    )(first, lo, hi, *scalars, inner)
    return turned(spread(out, groups)).reshape(rows, cells, columns)


def solution(mesh):
    return jax.shard_map(
        per_device,
        mesh=mesh,
        in_specs=(
            P("band", "lon", None),
            P("band", None),
            P(None, "band", None),
            P("band", None),
            P(None, "band", None),
        ),
        out_specs=P("band", "lon", None),
        check_vma=False,
    )
```

```python
import functools

import jax
import jax.numpy as jnp
from jax import lax
from jax.experimental import pallas as pl
from jax.experimental.pallas import tpu as pltpu
from jax.sharding import PartitionSpec as P

TMAX = 6
REACH = 8
VMEM = pltpu.VMEM
SMEM = pltpu.SMEM
DMA = pltpu.SemaphoreType.DMA
PARAMS = pltpu.CompilerParams(vmem_limit_bytes=8 * 1024 * 1024)


def columns_first(x_ref, lo, o_ref, place):
    groups, per_block, _ = o_ref.shape
    o_ref[:, :, place : place + 128] = x_ref[lo : lo + 128, :].T.reshape(groups, per_block, 128)


def rows_first(x_ref, place):
    groups, per_block, _ = x_ref.shape
    return x_ref[:, :, place : place + 128].reshape(groups * per_block, 128).T


def split_kernel(x_ref, *refs):
    count = (len(refs) - 4) // 2
    o_ref = refs[count]
    in_ref, x_sem, t_sem = refs[-3:]
    blocks = x_ref.shape[0] // 128
    copies = []
    for i in range(blocks):
        block = pl.ds(i * 128, 128)
        copies.append(pltpu.make_async_copy(x_ref.at[block], in_ref.at[block], x_sem.at[i]))
        copies[-1].start()
    tables = []
    for i in range(count):
        tables.append(pltpu.make_async_copy(refs[i], refs[count + 1 + i], t_sem.at[i]))
        tables[-1].start()
    for i in range(blocks):
        copies[i].wait()
        columns_first(in_ref, i * 128, o_ref, i * 128)
    for copy in tables:
        copy.wait()


def last_kernel(x_ref, o_ref, out_ref, sem):
    copies = []
    for i in range(out_ref.shape[0] // 128):
        block = pl.ds(i * 128, 128)
        out_ref[i * 128 : (i + 1) * 128, :] = rows_first(x_ref, i * 128)
        copies.append(pltpu.make_async_copy(out_ref.at[block], o_ref.at[block], sem.at[i]))
        copies[-1].start()
    for copy in copies:
        copy.wait()


def rotate(line, offset, weights, ext_ref, cells, lanes_per_block):
    lanes = line.shape[1]
    circle = lanes // lanes_per_block * cells
    wrapped = offset & (circle - 1)
    rest = wrapped & (cells - 1)
    step = (wrapped >> (cells.bit_length() - 1)) * lanes_per_block
    before = (step + lanes_per_block) & (lanes - 1)
    after = (step + lanes - lanes_per_block) & (lanes - 1)
    ext_ref[0:cells] = pltpu.roll(line, before, 1)
    ext_ref[cells : 2 * cells] = pltpu.roll(line, step, 1)
    ext_ref[2 * cells : 2 * cells + 8] = pltpu.roll(line[0:8], after, 1)
    total = None
    for k in range(4):
        term = weights[k] * ext_ref[pl.ds(cells - 1 - rest + k, cells), :]
        total = term if total is None else total + term
    return total


def level_here(levels):
    return lax.div(lax.axis_index("lon") * levels, lax.axis_size("lon"))


def first_pass(x_ref, place, row, level, off_ref, w_ref, turn_ref, ext_ref, cells, outs):
    per_block = x_ref.shape[1]
    turn_ref[...] = rows_first(x_ref, place)
    for i in range(128 // cells):
        r = row + i
        value = rotate(
            turn_ref[i * cells : (i + 1) * cells, :],
            off_ref[level, r],
            [w_ref[k, level, r] for k in range(4)],
            ext_ref.at[r],
            cells,
            per_block,
        )
        for ref, start in outs:
            ref[start + i * cells : start + (i + 1) * cells, :] = value


def edge_kernel(cells, levels, rows, x_ref, off_ref, w_ref, head_ref, tail_ref, turn_ref, ext_ref):
    level = level_here(levels)
    for j, (row, ref) in enumerate(((0, head_ref), (rows - REACH, tail_ref))):
        first_pass(x_ref, row * cells, row, level, off_ref, w_ref, turn_ref.at[j], ext_ref, cells, [(ref, 0)])


def rows_done(chosen, rows, cells, levels, source_ref, first_place, scalars, o_ref, turn_ref, ext_ref):
    off_ref, w_ref, toff_ref, tw_ref = scalars
    level = level_here(levels)
    first_row = lax.axis_index("band") * rows
    last_row = lax.axis_size("band") * rows - 1
    for r in chosen:
        shift = toff_ref[level, r]
        total = None
        for k in range(4):
            source = jnp.clip(first_row + (r + k - 1) - shift, 0, last_row) - first_row - first_place
            term = tw_ref[k, level, r] * source_ref[pl.ds(pl.multiple_of(source * cells, cells), cells), :]
            total = term if total is None else total + term
        turn_ref[r * cells : (r + 1) * cells, :] = rotate(
            total, off_ref[level, r], [w_ref[k, level, r] for k in range(4)], ext_ref.at[r], cells, o_ref.shape[1]
        )
    per_turn = 128 // cells
    for i in sorted({r // per_turn for r in chosen}):
        columns_first(turn_ref, i * 128, o_ref, i * 128)


def inner_kernel(
    cells, levels, x_ref, head_ref, tail_ref, off_ref, w_ref, toff_ref, tw_ref, o_ref, near_ref, all_ref, turn_ref, ext_ref
):
    flat = o_ref.shape[2]
    rows = flat // cells
    edge = REACH * cells
    level = level_here(levels)
    all_ref[0:edge] = head_ref[...]
    all_ref[flat - edge : flat] = tail_ref[...]
    for place in range(edge, flat - edge, 128):
        outs = [(all_ref, place)]
        if place < 2 * edge:
            outs.append((near_ref, place - edge))
        if place >= flat - 2 * edge:
            outs.append((near_ref, place - (flat - 2 * edge) + edge))
        turn = turn_ref.at[place : place + 128]
        first_pass(x_ref, place, place // cells, level, off_ref, w_ref, turn, ext_ref, cells, outs)
    scalars = (off_ref, w_ref, toff_ref, tw_ref)
    rows_done(range(REACH, rows - REACH), rows, cells, levels, all_ref, 0, scalars, o_ref, turn_ref, ext_ref)


def outer_kernel(
    cells, levels, lo_ref, head_ref, near_ref, tail_ref, hi_ref, off_ref, w_ref, toff_ref, tw_ref, i_ref, o_ref, all_ref, turn_ref, ext_ref
):
    flat = o_ref.shape[2]
    rows = flat // cells
    edge = REACH * cells
    scalars = (off_ref, w_ref, toff_ref, tw_ref)
    all_ref[0:edge] = lo_ref[...]
    all_ref[edge : 2 * edge] = head_ref[...]
    all_ref[2 * edge : 3 * edge] = near_ref[0:edge]
    all_ref[flat - edge : flat] = near_ref[edge : 2 * edge]
    all_ref[flat : flat + edge] = tail_ref[...]
    all_ref[flat + edge : flat + 2 * edge] = hi_ref[...]
    chosen = [*range(REACH), *range(rows - REACH, rows)]
    rows_done(chosen, rows, cells, levels, all_ref, -REACH, scalars, o_ref, turn_ref, ext_ref)


def exchanged(x):
    return lax.all_to_all(x, "lon", 0, 0, tiled=True)


def per_device(tracers, lon_offset, lon_weights, lat_offset, lat_weights):
    rows, cells, columns = tracers.shape
    levels = lon_offset.shape[1]
    groups = lax.axis_size("lon")
    per_block = columns // groups
    bands = lax.axis_size("band")
    flat = rows * cells
    edge = REACH * cells
    f32 = jnp.float32
    vspec = pl.BlockSpec(memory_space=VMEM)
    sspec = pl.BlockSpec(memory_space=SMEM)
    scalars = (lon_offset.T, lon_weights.transpose(0, 2, 1), lat_offset.T, lat_weights.transpose(0, 2, 1))
    ext = VMEM((rows, 2 * cells + 8, columns), f32)

    def slabs(*lanes):
        return [jax.ShapeDtypeStruct((groups, per_block, n), f32) for n in lanes]

    def lines(*counts):
        return [jax.ShapeDtypeStruct((n, columns), f32) for n in counts]

    spread, *scalars = pl.pallas_call(
        split_kernel,
        out_shape=slabs(flat) + [jax.ShapeDtypeStruct(x.shape, x.dtype) for x in scalars],
        in_specs=[pl.BlockSpec(memory_space=pltpu.HBM)] * 5,
        out_specs=[vspec] * 5,
        scratch_shapes=[VMEM((flat, columns), f32), DMA((flat // 128,)), DMA((4,))],
        compiler_params=PARAMS,
        name="split",
    )(*(pltpu.with_memory_space_constraint(x, pltpu.HBM) for x in (tracers.reshape(flat, columns), *scalars)))
    gathered = exchanged(spread)
    head, tail = pl.pallas_call(
        functools.partial(edge_kernel, cells, levels, rows),
        out_shape=lines(edge, edge),
        in_specs=[vspec, sspec, sspec],
        out_specs=[vspec] * 2,
        scratch_shapes=[VMEM((2, 128, columns), f32), ext],
        compiler_params=PARAMS,
        name="edge",
    )(gathered, *scalars[:2])
    lo = lax.ppermute(tail, "band", [(i, i + 1) for i in range(bands - 1)])
    hi = lax.ppermute(head, "band", [(i + 1, i) for i in range(bands - 1)])
    inner, near = pl.pallas_call(
        functools.partial(inner_kernel, cells, levels),
        out_shape=slabs(flat) + lines(2 * edge),
        in_specs=[vspec] * 3 + [sspec] * 4,
        out_specs=[vspec] * 2,
        scratch_shapes=[VMEM((flat, columns), f32), VMEM((flat, columns), f32), ext],
        compiler_params=PARAMS,
        name="inner",
    )(gathered, head, tail, *scalars)
    (out,) = pl.pallas_call(
        functools.partial(outer_kernel, cells, levels),
        out_shape=slabs(flat),
        in_specs=[vspec] * 5 + [sspec] * 4 + [vspec],
        out_specs=[vspec],
        scratch_shapes=[VMEM((flat + 2 * edge, columns), f32), VMEM((flat, columns), f32), ext],
        input_output_aliases={9: 0},
        compiler_params=PARAMS,
        name="outer",
    )(lo, head, near, tail, hi, *scalars, inner)
    (last,) = pl.pallas_call(
        last_kernel,
        out_shape=lines(flat),
        in_specs=[vspec],
        out_specs=[pl.BlockSpec(memory_space=pltpu.HBM)],
        scratch_shapes=[VMEM((flat, columns), f32), DMA((flat // 128,))],
        compiler_params=PARAMS,
        name="last",
    )(exchanged(out))
    return last.reshape(rows, cells, columns)


def solution(mesh):
    return jax.shard_map(
        per_device,
        mesh=mesh,
        in_specs=(
            P("band", "lon", None),
            P("band", None),
            P(None, "band", None),
            P("band", None),
            P(None, "band", None),
        ),
        out_specs=P("band", "lon", None),
        check_vma=False,
    )
```

```python
import functools

import jax
import jax.numpy as jnp
from jax import lax
from jax.experimental import pallas as pl
from jax.experimental.pallas import tpu as pltpu
from jax.sharding import PartitionSpec as P

TMAX = 6
REACH = 8
VMEM = pltpu.VMEM
SMEM = pltpu.SMEM
DMA = pltpu.SemaphoreType.DMA
PARAMS = pltpu.CompilerParams(vmem_limit_bytes=8 * 1024 * 1024)


def columns_first(x_ref, lo, o_ref, place):
    groups, per_block, _ = o_ref.shape
    o_ref[:, :, place : place + 128] = x_ref[lo : lo + 128, :].T.reshape(groups, per_block, 128)


def rows_first(x_ref, place):
    groups, per_block, _ = x_ref.shape
    return x_ref[:, :, place : place + 128].reshape(groups * per_block, 128).T


def split_kernel(x_ref, *refs):
    count = (len(refs) - 4) // 2
    o_ref = refs[count]
    in_ref, x_sem, t_sem = refs[-3:]
    blocks = x_ref.shape[0] // 128
    copies = []
    for i in range(blocks):
        block = pl.ds(i * 128, 128)
        copies.append(pltpu.make_async_copy(x_ref.at[block], in_ref.at[block], x_sem.at[i]))
        copies[-1].start()
    tables = []
    for i in range(count):
        tables.append(pltpu.make_async_copy(refs[i], refs[count + 1 + i], t_sem.at[i]))
        tables[-1].start()
    for i in range(blocks):
        copies[i].wait()
        columns_first(in_ref, i * 128, o_ref, i * 128)
    for copy in tables:
        copy.wait()


def last_kernel(x_ref, o_ref, out_ref, sem):
    copies = []
    for i in range(out_ref.shape[0] // 128):
        block = pl.ds(i * 128, 128)
        out_ref[i * 128 : (i + 1) * 128, :] = rows_first(x_ref, i * 128)
        copies.append(pltpu.make_async_copy(out_ref.at[block], o_ref.at[block], sem.at[i]))
        copies[-1].start()
    for copy in copies:
        copy.wait()


def rotate(line, offset, weights, ext_ref, cells, lanes_per_block):
    lanes = line.shape[1]
    circle = lanes // lanes_per_block * cells
    wrapped = offset & (circle - 1)
    rest = wrapped & (cells - 1)
    step = (wrapped >> (cells.bit_length() - 1)) * lanes_per_block
    before = (step + lanes_per_block) & (lanes - 1)
    after = (step + lanes - lanes_per_block) & (lanes - 1)
    ext_ref[0:cells] = pltpu.roll(line, before, 1)
    ext_ref[cells : 2 * cells] = pltpu.roll(line, step, 1)
    ext_ref[2 * cells : 2 * cells + 8] = pltpu.roll(line[0:8], after, 1)
    total = None
    for k in range(4):
        term = weights[k] * ext_ref[pl.ds(cells - 1 - rest + k, cells), :]
        total = term if total is None else total + term
    return total


def level_here(levels):
    return lax.div(lax.axis_index("lon") * levels, lax.axis_size("lon"))


def first_pass(x_ref, place, row, level, off_ref, w_ref, turn_ref, ext_ref, cells, outs):
    per_block = x_ref.shape[1]
    turn_ref[...] = rows_first(x_ref, place)
    for i in range(128 // cells):
        r = row + i
        value = rotate(
            turn_ref[i * cells : (i + 1) * cells, :],
            off_ref[level, r],
            [w_ref[k, level, r] for k in range(4)],
            ext_ref.at[r],
            cells,
            per_block,
        )
        for ref, start in outs:
            ref[start + i * cells : start + (i + 1) * cells, :] = value


def edge_kernel(cells, levels, rows, x_ref, off_ref, w_ref, head_ref, tail_ref, turn_ref, ext_ref):
    level = level_here(levels)
    for j, (row, ref) in enumerate(((0, head_ref), (rows - REACH, tail_ref))):
        first_pass(x_ref, row * cells, row, level, off_ref, w_ref, turn_ref.at[j], ext_ref, cells, [(ref, 0)])


def rows_done(chosen, rows, cells, levels, source_ref, first_place, scalars, o_ref, turn_ref, ext_ref):
    off_ref, w_ref, toff_ref, tw_ref = scalars
    level = level_here(levels)
    first_row = lax.axis_index("band") * rows
    last_row = lax.axis_size("band") * rows - 1
    for r in chosen:
        shift = toff_ref[level, r]
        total = None
        for k in range(4):
            source = jnp.clip(first_row + (r + k - 1) - shift, 0, last_row) - first_row - first_place
            term = tw_ref[k, level, r] * source_ref[pl.ds(pl.multiple_of(source * cells, cells), cells), :]
            total = term if total is None else total + term
        turn_ref[r * cells : (r + 1) * cells, :] = rotate(
            total, off_ref[level, r], [w_ref[k, level, r] for k in range(4)], ext_ref.at[r], cells, o_ref.shape[1]
        )
    per_turn = 128 // cells
    for i in sorted({r // per_turn for r in chosen}):
        columns_first(turn_ref, i * 128, o_ref, i * 128)


def inner_kernel(
    cells, levels, x_ref, head_ref, tail_ref, off_ref, w_ref, toff_ref, tw_ref, o_ref, near_ref, all_ref, turn_ref, ext_ref
):
    flat = o_ref.shape[2]
    rows = flat // cells
    edge = REACH * cells
    level = level_here(levels)
    all_ref[0:edge] = head_ref[...]
    all_ref[flat - edge : flat] = tail_ref[...]
    for place in range(edge, flat - edge, 128):
        outs = [(all_ref, place)]
        if place < 2 * edge:
            outs.append((near_ref, place - edge))
        if place >= flat - 2 * edge:
            outs.append((near_ref, place - (flat - 2 * edge) + edge))
        turn = turn_ref.at[place : place + 128]
        first_pass(x_ref, place, place // cells, level, off_ref, w_ref, turn, ext_ref, cells, outs)
    scalars = (off_ref, w_ref, toff_ref, tw_ref)
    rows_done(range(REACH, rows - REACH), rows, cells, levels, all_ref, 0, scalars, o_ref, turn_ref, ext_ref)


def outer_kernel(
    cells, levels, lo_ref, head_ref, near_ref, tail_ref, hi_ref, off_ref, w_ref, toff_ref, tw_ref, i_ref, o_ref, all_ref, turn_ref, ext_ref
):
    flat = o_ref.shape[2]
    rows = flat // cells
    edge = REACH * cells
    scalars = (off_ref, w_ref, toff_ref, tw_ref)
    all_ref[0:edge] = lo_ref[...]
    all_ref[edge : 2 * edge] = head_ref[...]
    all_ref[2 * edge : 3 * edge] = near_ref[0:edge]
    all_ref[flat - edge : flat] = near_ref[edge : 2 * edge]
    all_ref[flat : flat + edge] = tail_ref[...]
    all_ref[flat + edge : flat + 2 * edge] = hi_ref[...]
    chosen = [*range(REACH), *range(rows - REACH, rows)]
    rows_done(chosen, rows, cells, levels, all_ref, -REACH, scalars, o_ref, turn_ref, ext_ref)


def exchanged(x):
    return lax.all_to_all(x, "lon", 0, 0, tiled=True)


def per_device(tracers, lon_offset, lon_weights, lat_offset, lat_weights):
    rows, cells, columns = tracers.shape
    levels = lon_offset.shape[1]
    groups = lax.axis_size("lon")
    per_block = columns // groups
    bands = lax.axis_size("band")
    flat = rows * cells
    edge = REACH * cells
    f32 = jnp.float32
    vspec = pl.BlockSpec(memory_space=VMEM)
    sspec = pl.BlockSpec(memory_space=SMEM)
    scalars = (lon_offset.T, lon_weights.transpose(0, 2, 1), lat_offset.T, lat_weights.transpose(0, 2, 1))
    ext = VMEM((rows, 2 * cells + 8, columns), f32)

    def slabs(*lanes):
        return [jax.ShapeDtypeStruct((groups, per_block, n), f32) for n in lanes]

    def lines(*counts):
        return [jax.ShapeDtypeStruct((n, columns), f32) for n in counts]

    spread, *scalars = pl.pallas_call(
        split_kernel,
        out_shape=slabs(flat) + [SMEM(x.shape, x.dtype) for x in scalars],
        in_specs=[pl.BlockSpec(memory_space=pltpu.HBM)] * 5,
        out_specs=[vspec] + [sspec] * 4,
        scratch_shapes=[VMEM((flat, columns), f32), DMA((flat // 128,)), DMA((4,))],
        compiler_params=PARAMS,
        name="split",
    )(*(pltpu.with_memory_space_constraint(x, pltpu.HBM) for x in (tracers.reshape(flat, columns), *scalars)))
    scalars = [pltpu.with_memory_space_constraint(x, SMEM) for x in scalars]
    gathered = exchanged(spread)
    head, tail = pl.pallas_call(
        functools.partial(edge_kernel, cells, levels, rows),
        out_shape=lines(edge, edge),
        in_specs=[vspec, sspec, sspec],
        out_specs=[vspec] * 2,
        scratch_shapes=[VMEM((2, 128, columns), f32), ext],
        compiler_params=PARAMS,
        name="edge",
    )(gathered, *scalars[:2])
    lo = lax.ppermute(tail, "band", [(i, i + 1) for i in range(bands - 1)])
    hi = lax.ppermute(head, "band", [(i + 1, i) for i in range(bands - 1)])
    inner, near = pl.pallas_call(
        functools.partial(inner_kernel, cells, levels),
        out_shape=slabs(flat) + lines(2 * edge),
        in_specs=[vspec] * 3 + [sspec] * 4,
        out_specs=[vspec] * 2,
        scratch_shapes=[VMEM((flat, columns), f32), VMEM((flat, columns), f32), ext],
        compiler_params=PARAMS,
        name="inner",
    )(gathered, head, tail, *scalars)
    (out,) = pl.pallas_call(
        functools.partial(outer_kernel, cells, levels),
        out_shape=slabs(flat),
        in_specs=[vspec] * 5 + [sspec] * 4 + [vspec],
        out_specs=[vspec],
        scratch_shapes=[VMEM((flat + 2 * edge, columns), f32), VMEM((flat, columns), f32), ext],
        input_output_aliases={9: 0},
        compiler_params=PARAMS,
        name="outer",
    )(lo, head, near, tail, hi, *scalars, inner)
    (last,) = pl.pallas_call(
        last_kernel,
        out_shape=lines(flat),
        in_specs=[vspec],
        out_specs=[pl.BlockSpec(memory_space=pltpu.HBM)],
        scratch_shapes=[VMEM((flat, columns), f32), DMA((flat // 128,))],
        compiler_params=PARAMS,
        name="last",
    )(exchanged(out))
    return last.reshape(rows, cells, columns)


def solution(mesh):
    return jax.shard_map(
        per_device,
        mesh=mesh,
        in_specs=(
            P("band", "lon", None),
            P("band", None),
            P(None, "band", None),
            P("band", None),
            P(None, "band", None),
        ),
        out_specs=P("band", "lon", None),
        check_vma=False,
    )
```

```python
import functools

import jax
import jax.numpy as jnp
from jax import lax
from jax.experimental import pallas as pl
from jax.experimental.pallas import tpu as pltpu
from jax.sharding import PartitionSpec as P


REACH = 8
PARTS = 2
VMEM = pltpu.VMEM
SMEM = pltpu.SMEM
DMA = pltpu.SemaphoreType.DMA
PARAMS = pltpu.CompilerParams(vmem_limit_bytes=8 * 1024 * 1024)


def columns_first(block, groups):
    return block.T.reshape(groups, block.shape[1] // groups, block.shape[0])


def rows_first(slab):
    return slab.reshape(slab.shape[0] * slab.shape[1], slab.shape[2]).T


def split_kernel(x_ref, *refs):
    count = (len(refs) - 4) // 2
    o_ref = refs[count]
    in_ref, x_sem, t_sem = refs[-3:]
    pairs, cores, slabs, sets, per_set, _ = o_ref.shape
    part = x_ref.shape[0] // PARTS
    copies = []
    for i in range(PARTS):
        block = pl.ds(i * part, part)
        copies.append(pltpu.make_async_copy(x_ref.at[block], in_ref.at[block], x_sem.at[i]))
        copies[-1].start()
    tables = []
    for i in range(count):
        tables.append(pltpu.make_async_copy(refs[i], refs[count + 1 + i], t_sem.at[i]))
        tables[-1].start()
    for i in range(cores * slabs):
        if i * 128 % part == 0:
            copies[i * 128 // part].wait()
        value = columns_first(in_ref[i * 128 : (i + 1) * 128, :], pairs * sets).reshape(pairs, sets, per_set, 128)
        o_ref[:, i // slabs, i % slabs] = value
    for copy in tables:
        copy.wait()


def last_kernel(x_ref, o_ref, out_ref, sem):
    pairs, cores, slabs, sets, per_set, _ = x_ref.shape
    copies = []
    for i in range(cores * slabs):
        block = pl.ds(i * 128, 128)
        value = x_ref[:, i // slabs, i % slabs].reshape(pairs * sets, per_set, 128)
        out_ref[i * 128 : (i + 1) * 128, :] = rows_first(value)
        copies.append(pltpu.make_async_copy(out_ref.at[block], o_ref.at[block], sem.at[i]))
        copies[-1].start()
    for copy in copies:
        copy.wait()


def rotate(lines, offset, weights, ext_refs, cells, lanes_per_block):
    lanes = lines[0].shape[1]
    circle = lanes // lanes_per_block * cells
    wrapped = offset & (circle - 1)
    rest = wrapped & (cells - 1)
    step = (wrapped >> (cells.bit_length() - 1)) * lanes_per_block
    before = (step + lanes_per_block) & (lanes - 1)
    after = (step + lanes - lanes_per_block) & (lanes - 1)
    totals = []
    for line, ext_ref in zip(lines, ext_refs):
        ext_ref[0:cells] = pltpu.roll(line, before, 1)
        ext_ref[cells : 2 * cells] = pltpu.roll(line, step, 1)
        ext_ref[2 * cells : 2 * cells + 8] = pltpu.roll(line[0:8], after, 1)
        total = None
        for k in range(4):
            term = weights[k] * ext_ref[pl.ds(cells - 1 - rest + k, cells), :]
            total = term if total is None else total + term
        totals.append(total)
    return totals


def here(levels):
    lon = lax.axis_index("lon")
    return lax.div(lon * levels, lax.axis_size("lon")), lax.rem(lon, 2)


def first_pass(x_ref, slab, row, level, off_ref, w_ref, o_ref, turn_ref, ext_ref, cells):
    sets, per_set = x_ref.shape[2:4]
    for g in range(sets):
        turn_ref[g] = rows_first(x_ref[:, slab, g])
    for i in range(128 // cells):
        place = slice(i * cells, (i + 1) * cells)
        values = rotate(
            [turn_ref[g, place, :] for g in range(sets)],
            off_ref[level, row + i],
            [w_ref[k, level, row + i] for k in range(4)],
            [ext_ref.at[i, g] for g in range(sets)],
            cells,
            per_set,
        )
        for g in range(sets):
            o_ref[g * 128 + i * cells : g * 128 + (i + 1) * cells, :] = values[g]


def rows_done(slab, half, window_ref, first_place, level, core, tables, o_ref, turn_ref, ext_ref, cells):
    off_ref, w_ref, toff_ref, tw_ref = tables
    groups, _, sets, per_set, _ = o_ref.shape
    rows = 2 * half
    per_slab = 128 // cells
    first_row = lax.axis_index("band") * rows
    last_row = lax.axis_size("band") * rows - 1
    half_row = core * half
    for i in range(per_slab):
        row = half_row + slab * per_slab + i
        shift = toff_ref[level, row]
        totals = [None] * sets
        for k in range(4):
            source = jnp.clip(first_row + row + (k - 1) - shift, 0, last_row) - first_row - half_row - first_place
            weight = tw_ref[k, level, row]
            where = pl.ds(pl.multiple_of(source * cells, cells), cells)
            for g in range(sets):
                term = weight * window_ref[g, where, :]
                totals[g] = term if totals[g] is None else totals[g] + term
        values = rotate(
            totals,
            off_ref[level, row],
            [w_ref[k, level, row] for k in range(4)],
            [ext_ref.at[per_slab + i, g] for g in range(sets)],
            cells,
            per_set,
        )
        for g in range(sets):
            turn_ref[g, i * cells : (i + 1) * cells, :] = values[g]
    for g in range(sets):
        o_ref[:, slab, g] = columns_first(turn_ref[g], groups)


def edge_kernel(cells, levels, half, far, x_ref, off_ref, w_ref, o_ref, turn_ref, ext_ref):
    level, core = here(levels)
    slab = (core if far else 1 - core) * (x_ref.shape[1] - 1)
    row = core * half + slab * (128 // cells)
    first_pass(x_ref, slab, row, level, off_ref, w_ref, o_ref, turn_ref, ext_ref, cells)


def inner_kernel(
    cells, levels, half, x_ref, far_ref, near_ref, off_ref, w_ref, toff_ref, tw_ref, o_ref, mid_ref, own_ref, turn_ref, ext_ref
):
    level, core = here(levels)
    sets = x_ref.shape[2]
    row = core * half + 128 // cells
    first_pass(x_ref, 1, row, level, off_ref, w_ref, mid_ref, turn_ref, ext_ref, cells)
    for g in range(sets):
        part = slice(g * 128, (g + 1) * 128)
        own_ref[g, pl.ds(pl.multiple_of(core * 256, 128), 128), :] = far_ref[part, :]
        own_ref[g, 128:256, :] = mid_ref[part, :]
        own_ref[g, pl.ds(pl.multiple_of((1 - core) * 256, 128), 128), :] = near_ref[part, :]
    tables = (off_ref, w_ref, toff_ref, tw_ref)
    rows_done(1, half, own_ref, 0, level, core, tables, o_ref, turn_ref, ext_ref, cells)


def side_kernel(
    cells, levels, half, far, edge_ref, mid_ref, halo_ref, off_ref, w_ref, toff_ref, tw_ref, i_ref, o_ref, own_ref, turn_ref, ext_ref
):
    level, core = here(levels)
    above = 1 - core if far else core
    sets = o_ref.shape[2]
    for g in range(sets):
        part = slice(g * 128, (g + 1) * 128)
        own_ref[g, pl.ds(pl.multiple_of((1 - above) * 256, 128), 128), :] = halo_ref[part, :]
        own_ref[g, 128:256, :] = edge_ref[part, :]
        own_ref[g, pl.ds(pl.multiple_of(above * 256, 128), 128), :] = mid_ref[part, :]
    slab = (1 - above) * 2
    first_place = (slab - 1) * (128 // cells)
    tables = (off_ref, w_ref, toff_ref, tw_ref)
    rows_done(slab, half, own_ref, first_place, level, core, tables, o_ref, turn_ref, ext_ref, cells)


def exchanged(x):
    return lax.all_to_all(x, "lon", 0, 0, tiled=True)


def per_device(tracers, lon_offset, lon_weights, lat_offset, lat_weights):
    rows, cells, columns = tracers.shape
    levels = lon_offset.shape[1]
    groups = lax.axis_size("lon")
    bands = lax.axis_size("band")
    flat = rows * cells
    half = rows // 2
    slabs = half * cells // 128
    per_set = 128 // groups
    sets = columns * 2 // groups // per_set
    f32 = jnp.float32
    vspec = pl.BlockSpec(memory_space=VMEM)
    sspec = pl.BlockSpec(memory_space=SMEM)
    hspec = pl.BlockSpec(memory_space=pltpu.HBM)
    tables = (lon_offset.T, lon_weights.transpose(0, 2, 1), lat_offset.T, lat_weights.transpose(0, 2, 1))
    assert slabs == 3 and REACH * cells == 128 and columns == 128
    sent = jax.ShapeDtypeStruct((groups // 2, 2, slabs, sets, per_set, 128), f32)
    slab_lines = jax.ShapeDtypeStruct((sets * 128, 128), f32)
    gathered_shape = (groups, *sent.shape[2:])
    turn = VMEM((sets, 128, 128), f32)
    ext = VMEM((2 * 128 // cells, sets, 2 * cells + 8, 128), f32)
    own = VMEM((sets, 3 * 128, 128), f32)

    def call(kernel, out_shape, in_specs, scratch, *args, aliases={}):
        return pl.pallas_call(
            kernel,
            out_shape=out_shape,
            in_specs=in_specs,
            out_specs=jax.tree.map(lambda x: vspec if isinstance(x, jax.ShapeDtypeStruct) else sspec, out_shape),
            scratch_shapes=scratch,
            input_output_aliases=aliases,
            compiler_params=PARAMS,
        )(*args)

    given = [pltpu.with_memory_space_constraint(x, pltpu.HBM) for x in (tracers.reshape(flat, columns), *tables)]
    spread, *tables = call(
        split_kernel,
        [sent] + [SMEM(x.shape, x.dtype) for x in tables],
        [hspec] * 5,
        [VMEM((flat, columns), f32), DMA((PARTS,)), DMA((4,))],
        *given,
    )
    tables = [pltpu.with_memory_space_constraint(x, SMEM) for x in tables]
    gathered = exchanged(spread.reshape(gathered_shape))

    def edge(far):
        kernel = functools.partial(edge_kernel, cells, levels, half, far)
        return call(kernel, slab_lines, [vspec, sspec, sspec], [turn, ext], gathered, *tables[:2])

    far = edge(True)
    pairs = []
    for n in range(bands - 1):
        for lon in range(1, groups, 2):
            lower, upper = n * groups + lon, (n + 1) * groups + lon - 1
            pairs += [(lower, upper), (upper, lower)]
    far_halo = lax.ppermute(far, ("band", "lon"), pairs)
    near = edge(False)
    near_halo = lax.ppermute(near, "lon", [(lon, lon ^ 1) for lon in range(groups)])
    out, mid = call(
        functools.partial(inner_kernel, cells, levels, half),
        [jax.ShapeDtypeStruct(gathered_shape, f32), slab_lines],
        [vspec] * 3 + [sspec] * 4,
        [own, turn, ext],
        gathered,
        far,
        near,
        *tables,
    )
    for is_far, edge_rows, halo in ((False, near, near_halo), (True, far, far_halo)):
        out = call(
            functools.partial(side_kernel, cells, levels, half, is_far),
            jax.ShapeDtypeStruct(gathered_shape, f32),
            [vspec] * 3 + [sspec] * 4 + [vspec],
            [own, turn, ext],
            edge_rows,
            mid,
            halo,
            *tables,
            out,
            aliases={7: 0},
        )
    last = pl.pallas_call(
        last_kernel,
        out_shape=jax.ShapeDtypeStruct((flat, columns), f32),
        in_specs=[vspec],
        out_specs=hspec,
        scratch_shapes=[VMEM((flat, columns), f32), DMA((flat // 128,))],
        compiler_params=PARAMS,
        name="last",
    )(exchanged(out).reshape(sent.shape))
    return last.reshape(rows, cells, columns)


def solution(mesh):
    return jax.shard_map(
        per_device,
        mesh=mesh,
        in_specs=(
            P("band", "lon", None),
            P("band", None),
            P(None, "band", None),
            P("band", None),
            P(None, "band", None),
        ),
        out_specs=P("band", "lon", None),
        check_vma=False,
    )
```

```python
import functools

import jax
import jax.numpy as jnp
from jax import lax
from jax.experimental import pallas as pl
from jax.experimental.pallas import tpu as pltpu
from jax.sharding import PartitionSpec as P


REACH = 8
PARTS = 2
VMEM = pltpu.VMEM
SMEM = pltpu.SMEM
DMA = pltpu.SemaphoreType.DMA
PARAMS = pltpu.CompilerParams(vmem_limit_bytes=8 * 1024 * 1024)


def columns_first(block, groups):
    return block.T.reshape(groups, block.shape[1] // groups, block.shape[0])


def rows_first(slab):
    return slab.reshape(slab.shape[0] * slab.shape[1], slab.shape[2]).T


def split_kernel(x_ref, *refs):
    count = (len(refs) - 4) // 2
    o_ref = refs[count]
    in_ref, x_sem, t_sem = refs[-3:]
    pairs, cores, slabs, sets, per_set, _ = o_ref.shape
    part = x_ref.shape[0] // PARTS
    copies = []
    for i in range(PARTS):
        block = pl.ds(i * part, part)
        copies.append(pltpu.make_async_copy(x_ref.at[block], in_ref.at[block], x_sem.at[i]))
        copies[-1].start()
    tables = []
    for i in range(count):
        tables.append(pltpu.make_async_copy(refs[i], refs[count + 1 + i], t_sem.at[i]))
        tables[-1].start()
    for i in range(cores * slabs):
        if i * 128 % part == 0:
            copies[i * 128 // part].wait()
        value = columns_first(in_ref[i * 128 : (i + 1) * 128, :], pairs * sets).reshape(pairs, sets, per_set, 128)
        o_ref[:, i // slabs, i % slabs] = value
    for copy in tables:
        copy.wait()


def last_kernel(x_ref, o_ref, out_ref, sem):
    pairs, cores, slabs, sets, per_set, _ = x_ref.shape
    copies = []
    for i in range(cores * slabs):
        block = pl.ds(i * 128, 128)
        value = x_ref[:, i // slabs, i % slabs].reshape(pairs * sets, per_set, 128)
        out_ref[i * 128 : (i + 1) * 128, :] = rows_first(value)
        copies.append(pltpu.make_async_copy(out_ref.at[block], o_ref.at[block], sem.at[i]))
        copies[-1].start()
    for copy in copies:
        copy.wait()


def rotate(lines, offset, weights, ext_refs, cells, lanes_per_block):
    lanes = lines[0].shape[1]
    circle = lanes // lanes_per_block * cells
    wrapped = offset & (circle - 1)
    rest = wrapped & (cells - 1)
    step = (wrapped >> (cells.bit_length() - 1)) * lanes_per_block
    before = (step + lanes_per_block) & (lanes - 1)
    after = (step + lanes - lanes_per_block) & (lanes - 1)
    totals = []
    for line, ext_ref in zip(lines, ext_refs):
        ext_ref[0:cells] = pltpu.roll(line, before, 1)
        ext_ref[cells : 2 * cells] = pltpu.roll(line, step, 1)
        ext_ref[2 * cells : 2 * cells + 8] = pltpu.roll(line[0:8], after, 1)
        total = None
        for k in range(4):
            term = weights[k] * ext_ref[pl.ds(cells - 1 - rest + k, cells), :]
            total = term if total is None else total + term
        totals.append(total)
    return totals


def here(levels):
    lon = lax.axis_index("lon")
    return lax.div(lon * levels, lax.axis_size("lon")), lax.rem(lon, 2)


def first_pass(x_ref, slab, row, level, off_ref, w_ref, o_ref, turn_ref, ext_ref, cells):
    sets, per_set = x_ref.shape[2:4]
    for g in range(sets):
        turn_ref[g] = rows_first(x_ref[:, slab, g])
    for i in range(128 // cells):
        place = slice(i * cells, (i + 1) * cells)
        values = rotate(
            [turn_ref[g, place, :] for g in range(sets)],
            off_ref[level, row + i],
            [w_ref[k, level, row + i] for k in range(4)],
            [ext_ref.at[i, g] for g in range(sets)],
            cells,
            per_set,
        )
        for g in range(sets):
            o_ref[g * 128 + i * cells : g * 128 + (i + 1) * cells, :] = values[g]


def rows_done(slab, half, window_ref, first_place, level, core, tables, o_ref, turn_ref, ext_ref, cells):
    off_ref, w_ref, toff_ref, tw_ref = tables
    groups, _, sets, per_set, _ = o_ref.shape
    rows = 2 * half
    per_slab = 128 // cells
    first_row = lax.axis_index("band") * rows
    last_row = lax.axis_size("band") * rows - 1
    half_row = core * half
    for i in range(per_slab):
        row = half_row + slab * per_slab + i
        shift = toff_ref[level, row]
        totals = [None] * sets
        for k in range(4):
            source = jnp.clip(first_row + row + (k - 1) - shift, 0, last_row) - first_row - half_row - first_place
            weight = tw_ref[k, level, row]
            where = pl.ds(pl.multiple_of(source * cells, cells), cells)
            for g in range(sets):
                term = weight * window_ref[g, where, :]
                totals[g] = term if totals[g] is None else totals[g] + term
        values = rotate(
            totals,
            off_ref[level, row],
            [w_ref[k, level, row] for k in range(4)],
            [ext_ref.at[per_slab + i, g] for g in range(sets)],
            cells,
            per_set,
        )
        for g in range(sets):
            turn_ref[g, i * cells : (i + 1) * cells, :] = values[g]
    for g in range(sets):
        o_ref[:, slab, g] = columns_first(turn_ref[g], groups)


def edge_kernel(cells, levels, half, far, x_ref, off_ref, w_ref, o_ref, turn_ref, ext_ref):
    level, core = here(levels)
    slab = (core if far else 1 - core) * (x_ref.shape[1] - 1)
    row = core * half + slab * (128 // cells)
    first_pass(x_ref, slab, row, level, off_ref, w_ref, o_ref, turn_ref, ext_ref, cells)


def inner_kernel(
    cells, levels, half, x_ref, far_ref, near_ref, off_ref, w_ref, toff_ref, tw_ref, o_ref, mid_ref, own_ref, turn_ref, ext_ref
):
    level, core = here(levels)
    sets = x_ref.shape[2]
    row = core * half + 128 // cells
    first_pass(x_ref, 1, row, level, off_ref, w_ref, mid_ref, turn_ref, ext_ref, cells)
    for g in range(sets):
        part = slice(g * 128, (g + 1) * 128)
        own_ref[g, pl.ds(pl.multiple_of(core * 256, 128), 128), :] = far_ref[part, :]
        own_ref[g, 128:256, :] = mid_ref[part, :]
        own_ref[g, pl.ds(pl.multiple_of((1 - core) * 256, 128), 128), :] = near_ref[part, :]
    tables = (off_ref, w_ref, toff_ref, tw_ref)
    rows_done(1, half, own_ref, 0, level, core, tables, o_ref, turn_ref, ext_ref, cells)


def side_kernel(
    cells, levels, half, far, edge_ref, mid_ref, halo_ref, off_ref, w_ref, toff_ref, tw_ref, i_ref, o_ref, own_ref, turn_ref, ext_ref
):
    level, core = here(levels)
    above = 1 - core if far else core
    sets = o_ref.shape[2]
    for g in range(sets):
        part = slice(g * 128, (g + 1) * 128)
        halo = halo_ref[part, :] if far else halo_ref[1 - core, part, :]
        own_ref[g, pl.ds(pl.multiple_of((1 - above) * 256, 128), 128), :] = halo
        own_ref[g, 128:256, :] = edge_ref[part, :]
        own_ref[g, pl.ds(pl.multiple_of(above * 256, 128), 128), :] = mid_ref[part, :]
    slab = (1 - above) * 2
    first_place = (slab - 1) * (128 // cells)
    tables = (off_ref, w_ref, toff_ref, tw_ref)
    rows_done(slab, half, own_ref, first_place, level, core, tables, o_ref, turn_ref, ext_ref, cells)


def exchanged(x):
    return lax.all_to_all(x, "lon", 0, 0, tiled=True)


def per_device(tracers, lon_offset, lon_weights, lat_offset, lat_weights):
    rows, cells, columns = tracers.shape
    levels = lon_offset.shape[1]
    groups = lax.axis_size("lon")
    bands = lax.axis_size("band")
    flat = rows * cells
    half = rows // 2
    slabs = half * cells // 128
    per_set = 128 // groups
    sets = columns * 2 // groups // per_set
    f32 = jnp.float32
    vspec = pl.BlockSpec(memory_space=VMEM)
    sspec = pl.BlockSpec(memory_space=SMEM)
    hspec = pl.BlockSpec(memory_space=pltpu.HBM)
    tables = (lon_offset.T, lon_weights.transpose(0, 2, 1), lat_offset.T, lat_weights.transpose(0, 2, 1))
    assert slabs == 3 and REACH * cells == 128 and columns == 128
    sent = jax.ShapeDtypeStruct((groups // 2, 2, slabs, sets, per_set, 128), f32)
    slab_lines = jax.ShapeDtypeStruct((sets * 128, 128), f32)
    gathered_shape = (groups, *sent.shape[2:])
    turn = VMEM((sets, 128, 128), f32)
    ext = VMEM((2 * 128 // cells, sets, 2 * cells + 8, 128), f32)
    own = VMEM((sets, 3 * 128, 128), f32)

    def call(kernel, out_shape, in_specs, scratch, *args, aliases={}):
        return pl.pallas_call(
            kernel,
            out_shape=out_shape,
            in_specs=in_specs,
            out_specs=jax.tree.map(lambda x: vspec if isinstance(x, jax.ShapeDtypeStruct) else sspec, out_shape),
            scratch_shapes=scratch,
            input_output_aliases=aliases,
            compiler_params=PARAMS,
        )(*args)

    given = [pltpu.with_memory_space_constraint(x, pltpu.HBM) for x in (tracers.reshape(flat, columns), *tables)]
    spread, *tables = call(
        split_kernel,
        [sent] + [SMEM(x.shape, x.dtype) for x in tables],
        [hspec] * 5,
        [VMEM((flat, columns), f32), DMA((PARTS,)), DMA((4,))],
        *given,
    )
    tables = [pltpu.with_memory_space_constraint(x, SMEM) for x in tables]
    gathered = exchanged(spread.reshape(gathered_shape))

    def edge(far):
        kernel = functools.partial(edge_kernel, cells, levels, half, far)
        return call(kernel, slab_lines, [vspec, sspec, sspec], [turn, ext], gathered, *tables[:2])

    far = edge(True)
    pairs = []
    for n in range(bands - 1):
        for lon in range(1, groups, 2):
            lower, upper = n * groups + lon, (n + 1) * groups + lon - 1
            pairs += [(lower, upper), (upper, lower)]
    far_halo = lax.ppermute(far, ("band", "lon"), pairs)
    near = edge(False)
    near_halo = lax.all_gather(near, "lon", axis_index_groups=[[lon, lon + 1] for lon in range(0, groups, 2)])
    out, mid = call(
        functools.partial(inner_kernel, cells, levels, half),
        [jax.ShapeDtypeStruct(gathered_shape, f32), slab_lines],
        [vspec] * 3 + [sspec] * 4,
        [own, turn, ext],
        gathered,
        far,
        near,
        *tables,
    )
    for is_far, edge_rows, halo in ((False, near, near_halo), (True, far, far_halo)):
        out = call(
            functools.partial(side_kernel, cells, levels, half, is_far),
            jax.ShapeDtypeStruct(gathered_shape, f32),
            [vspec] * 3 + [sspec] * 4 + [vspec],
            [own, turn, ext],
            edge_rows,
            mid,
            halo,
            *tables,
            out,
            aliases={7: 0},
        )
    last = pl.pallas_call(
        last_kernel,
        out_shape=jax.ShapeDtypeStruct((flat, columns), f32),
        in_specs=[vspec],
        out_specs=hspec,
        scratch_shapes=[VMEM((flat, columns), f32), DMA((flat // 128,))],
        compiler_params=PARAMS,
        name="last",
    )(exchanged(out).reshape(sent.shape))
    return last.reshape(rows, cells, columns)


def solution(mesh):
    return jax.shard_map(
        per_device,
        mesh=mesh,
        in_specs=(
            P("band", "lon", None),
            P("band", None),
            P(None, "band", None),
            P("band", None),
            P(None, "band", None),
        ),
        out_specs=P("band", "lon", None),
        check_vma=False,
    )
```

```python
import functools

import jax
import jax.numpy as jnp
from jax import lax
from jax.experimental import pallas as pl
from jax.experimental.pallas import tpu as pltpu
from jax.sharding import PartitionSpec as P


REACH = 8
PARTS = 1
VMEM = pltpu.VMEM
SMEM = pltpu.SMEM
DMA = pltpu.SemaphoreType.DMA
PARAMS = pltpu.CompilerParams(vmem_limit_bytes=8 * 1024 * 1024)


def columns_first(block, groups):
    return block.T.reshape(groups, block.shape[1] // groups, block.shape[0])


def rows_first(slab):
    return slab.reshape(slab.shape[0] * slab.shape[1], slab.shape[2]).T


def split_kernel(x_ref, *refs):
    count = (len(refs) - 4) // 2
    o_ref = refs[count]
    in_ref, x_sem, t_sem = refs[-3:]
    pairs, cores, slabs, sets, per_set, _ = o_ref.shape
    part = x_ref.shape[0] // PARTS
    copies = []
    for i in range(PARTS):
        block = pl.ds(i * part, part)
        copies.append(pltpu.make_async_copy(x_ref.at[block], in_ref.at[block], x_sem.at[i]))
        copies[-1].start()
    tables = []
    for i in range(count):
        tables.append(pltpu.make_async_copy(refs[i], refs[count + 1 + i], t_sem.at[i]))
        tables[-1].start()
    for i in range(cores * slabs):
        if i * 128 % part == 0:
            copies[i * 128 // part].wait()
        value = columns_first(in_ref[i * 128 : (i + 1) * 128, :], pairs * sets).reshape(pairs, sets, per_set, 128)
        o_ref[:, i // slabs, i % slabs] = value
    for copy in tables:
        copy.wait()


def last_kernel(x_ref, o_ref, out_ref, sem):
    pairs, cores, slabs, sets, per_set, _ = x_ref.shape
    copies = []
    for i in range(cores * slabs):
        block = pl.ds(i * 128, 128)
        value = x_ref[:, i // slabs, i % slabs].reshape(pairs * sets, per_set, 128)
        out_ref[i * 128 : (i + 1) * 128, :] = rows_first(value)
        copies.append(pltpu.make_async_copy(out_ref.at[block], o_ref.at[block], sem.at[i]))
        copies[-1].start()
    for copy in copies:
        copy.wait()


def placed(lines, offset, ext_refs, cells, lanes_per_block):
    lanes = lines[0].shape[1]
    circle = lanes // lanes_per_block * cells
    wrapped = offset & (circle - 1)
    step = (wrapped >> (cells.bit_length() - 1)) * lanes_per_block
    before = (step + lanes_per_block) & (lanes - 1)
    after = (step + lanes - lanes_per_block) & (lanes - 1)
    for line, ext_ref in zip(lines, ext_refs):
        ext_ref[0:cells] = pltpu.roll(line, before, 1)
        ext_ref[cells : 2 * cells] = pltpu.roll(line, step, 1)
        ext_ref[2 * cells : 2 * cells + 8] = pltpu.roll(line[0:8], after, 1)
    return cells - 1 - (wrapped & (cells - 1))


def tapped(start, weights, ext_refs, cells):
    totals = []
    for ext_ref in ext_refs:
        total = None
        for k in range(4):
            term = weights[k] * ext_ref[pl.ds(start + k, cells), :]
            total = term if total is None else total + term
        totals.append(total)
    return totals


def here(levels):
    lon = lax.axis_index("lon")
    return lax.div(lon * levels, lax.axis_size("lon")), lax.rem(lon, 2)


def first_pass(x_ref, slab, row, level, off_ref, w_ref, o_ref, turn_ref, ext_ref, cells):
    sets, per_set = x_ref.shape[2:4]
    for g in range(sets):
        turn_ref[g] = rows_first(x_ref[:, slab, g])
    count = 128 // cells
    exts = [[ext_ref[i].at[g] for g in range(sets)] for i in range(count)]
    starts = []
    for i in range(count):
        lines = [turn_ref[g, i * cells : (i + 1) * cells, :] for g in range(sets)]
        starts.append(placed(lines, off_ref[level, row + i], exts[i], cells, per_set))
    for i in range(count):
        values = tapped(starts[i], [w_ref[k, level, row + i] for k in range(4)], exts[i], cells)
        for g in range(sets):
            o_ref[g * 128 + i * cells : g * 128 + (i + 1) * cells, :] = values[g]


def rows_done(slab, half, window_ref, first_place, level, core, tables, o_ref, turn_ref, ext_ref, cells, use=1):
    off_ref, w_ref, toff_ref, tw_ref = tables
    groups, _, sets, per_set, _ = o_ref.shape
    rows = 2 * half
    per_slab = 128 // cells
    first_row = lax.axis_index("band") * rows
    last_row = lax.axis_size("band") * rows - 1
    half_row = core * half
    first = half_row + slab * per_slab
    exts = [[ext_ref[use * per_slab + i].at[g] for g in range(sets)] for i in range(per_slab)]
    starts = []
    for i in range(per_slab):
        row = first + i
        shift = toff_ref[level, row]
        totals = [None] * sets
        for k in range(4):
            source = jnp.clip(first_row + row + (k - 1) - shift, 0, last_row) - first_row - half_row - first_place
            weight = tw_ref[k, level, row]
            where = pl.ds(pl.multiple_of(source * cells, cells), cells)
            for g in range(sets):
                term = weight * window_ref[g, where, :]
                totals[g] = term if totals[g] is None else totals[g] + term
        starts.append(placed(totals, off_ref[level, row], exts[i], cells, per_set))
    for i in range(per_slab):
        values = tapped(starts[i], [w_ref[k, level, first + i] for k in range(4)], exts[i], cells)
        for g in range(sets):
            turn_ref[g, i * cells : (i + 1) * cells, :] = values[g]
    for g in range(sets):
        o_ref[:, slab, g] = columns_first(turn_ref[g], groups)


def edge_kernel(cells, levels, half, far, x_ref, off_ref, w_ref, o_ref, turn_ref, ext_ref):
    level, core = here(levels)
    slab = (core if far else 1 - core) * (x_ref.shape[1] - 1)
    row = core * half + slab * (128 // cells)
    first_pass(x_ref, slab, row, level, off_ref, w_ref, o_ref, turn_ref, ext_ref, cells)


def inner_kernel(
    cells, levels, half, x_ref, far_ref, near_ref, halo_ref, off_ref, w_ref, toff_ref, tw_ref, o_ref, mid_ref, own_ref, turn_ref, ext_ref
):
    level, core = here(levels)
    sets = x_ref.shape[2]
    row = core * half + 128 // cells
    first_pass(x_ref, 1, row, level, off_ref, w_ref, mid_ref, turn_ref, ext_ref, cells)
    for g in range(sets):
        part = slice(g * 128, (g + 1) * 128)
        own_ref[g, pl.ds(pl.multiple_of(128 + core * 256, 128), 128), :] = far_ref[part, :]
        own_ref[g, 256:384, :] = mid_ref[part, :]
        own_ref[g, pl.ds(pl.multiple_of(384 - core * 256, 128), 128), :] = near_ref[part, :]
        own_ref[g, pl.ds(pl.multiple_of(512 - core * 512, 128), 128), :] = halo_ref[1 - core, part, :]
    tables = (off_ref, w_ref, toff_ref, tw_ref)
    for use, slab in ((1, 1), (2, 2 - 2 * core)):
        rows_done(slab, half, own_ref, -(128 // cells), level, core, tables, o_ref, turn_ref, ext_ref, cells, use)


def outer_kernel(
    cells, levels, half, edge_ref, mid_ref, halo_ref, off_ref, w_ref, toff_ref, tw_ref, i_ref, o_ref, own_ref, turn_ref, ext_ref
):
    level, core = here(levels)
    for g in range(o_ref.shape[2]):
        part = slice(g * 128, (g + 1) * 128)
        own_ref[g, pl.ds(pl.multiple_of(core * 256, 128), 128), :] = halo_ref[part, :]
        own_ref[g, 128:256, :] = edge_ref[part, :]
        own_ref[g, pl.ds(pl.multiple_of((1 - core) * 256, 128), 128), :] = mid_ref[part, :]
    slab = core * 2
    first_place = (slab - 1) * (128 // cells)
    tables = (off_ref, w_ref, toff_ref, tw_ref)
    rows_done(slab, half, own_ref, first_place, level, core, tables, o_ref, turn_ref, ext_ref, cells)


def exchanged(x):
    return lax.all_to_all(x, "lon", 0, 0, tiled=True)


def per_device(tracers, lon_offset, lon_weights, lat_offset, lat_weights):
    rows, cells, columns = tracers.shape
    levels = lon_offset.shape[1]
    groups = lax.axis_size("lon")
    bands = lax.axis_size("band")
    flat = rows * cells
    half = rows // 2
    slabs = half * cells // 128
    per_set = 128 // groups
    sets = columns * 2 // groups // per_set
    f32 = jnp.float32
    vspec = pl.BlockSpec(memory_space=VMEM)
    sspec = pl.BlockSpec(memory_space=SMEM)
    hspec = pl.BlockSpec(memory_space=pltpu.HBM)
    tables = (lon_offset.T, lon_weights.transpose(0, 2, 1), lat_offset.T, lat_weights.transpose(0, 2, 1))
    assert slabs == 3 and REACH * cells == 128 and columns == 128
    sent = jax.ShapeDtypeStruct((groups // 2, 2, slabs, sets, per_set, 128), f32)
    slab_lines = jax.ShapeDtypeStruct((sets * 128, 128), f32)
    gathered_shape = (groups, *sent.shape[2:])
    turn = VMEM((sets, 128, 128), f32)
    ext = (VMEM((sets, 2 * cells + 8, 128), f32),) * (3 * 128 // cells)
    own = VMEM((sets, 3 * 128, 128), f32)

    def call(kernel, out_shape, in_specs, scratch, *args, aliases={}):
        return pl.pallas_call(
            kernel,
            out_shape=out_shape,
            in_specs=in_specs,
            out_specs=jax.tree.map(lambda x: vspec if isinstance(x, jax.ShapeDtypeStruct) else sspec, out_shape),
            scratch_shapes=scratch,
            input_output_aliases=aliases,
            compiler_params=PARAMS,
        )(*args)

    given = [pltpu.with_memory_space_constraint(x, pltpu.HBM) for x in (tracers.reshape(flat, columns), *tables)]
    spread, *tables = call(
        split_kernel,
        [sent] + [SMEM(x.shape, x.dtype) for x in tables],
        [hspec] * 5,
        [VMEM((flat, columns), f32), DMA((PARTS,)), DMA((4,))],
        *given,
    )
    tables = [pltpu.with_memory_space_constraint(x, SMEM) for x in tables]
    gathered = exchanged(spread.reshape(gathered_shape))

    def edge(far):
        kernel = functools.partial(edge_kernel, cells, levels, half, far)
        return call(kernel, slab_lines, [vspec, sspec, sspec], [turn, ext], gathered, *tables[:2])

    far = edge(True)
    pairs = []
    for n in range(bands - 1):
        for lon in range(1, groups, 2):
            lower, upper = n * groups + lon, (n + 1) * groups + lon - 1
            pairs += [(lower, upper), (upper, lower)]
    far_halo = lax.ppermute(far, ("band", "lon"), pairs)
    near = edge(False)
    near_halo = lax.all_gather(near, "lon", axis_index_groups=[[lon, lon + 1] for lon in range(0, groups, 2)])
    out, mid = call(
        functools.partial(inner_kernel, cells, levels, half),
        [jax.ShapeDtypeStruct(gathered_shape, f32), slab_lines],
        [vspec] * 4 + [sspec] * 4,
        [VMEM((sets, 5 * 128, 128), f32), turn, ext],
        gathered,
        far,
        near,
        near_halo,
        *tables,
    )
    out = call(
        functools.partial(outer_kernel, cells, levels, half),
        jax.ShapeDtypeStruct(gathered_shape, f32),
        [vspec] * 3 + [sspec] * 4 + [vspec],
        [own, turn, ext],
        far,
        mid,
        far_halo,
        *tables,
        out,
        aliases={7: 0},
    )
    last = pl.pallas_call(
        last_kernel,
        out_shape=jax.ShapeDtypeStruct((flat, columns), f32),
        in_specs=[vspec],
        out_specs=hspec,
        scratch_shapes=[VMEM((flat, columns), f32), DMA((flat // 128,))],
        compiler_params=PARAMS,
        name="last",
    )(exchanged(out).reshape(sent.shape))
    return last.reshape(rows, cells, columns)


def solution(mesh):
    return jax.shard_map(
        per_device,
        mesh=mesh,
        in_specs=(
            P("band", "lon", None),
            P("band", None),
            P(None, "band", None),
            P("band", None),
            P(None, "band", None),
        ),
        out_specs=P("band", "lon", None),
        check_vma=False,
    )
```

```python
import functools

import jax
import jax.numpy as jnp
from jax import lax
from jax.experimental import pallas as pl
from jax.experimental.pallas import tpu as pltpu
from jax.sharding import PartitionSpec as P


REACH = 8
PARTS = 1
VMEM = pltpu.VMEM
SMEM = pltpu.SMEM
DMA = pltpu.SemaphoreType.DMA
PARAMS = pltpu.CompilerParams(vmem_limit_bytes=8 * 1024 * 1024)


def columns_first(block, groups):
    return block.T.reshape(groups, block.shape[1] // groups, block.shape[0])


def rows_first(slab):
    return slab.reshape(slab.shape[0] * slab.shape[1], slab.shape[2]).T


def split_kernel(x_ref, *refs):
    count = (len(refs) - 4) // 2
    o_ref = refs[count]
    in_ref, x_sem, t_sem = refs[-3:]
    pairs, cores, slabs, _, _ = o_ref.shape
    part = x_ref.shape[0] // PARTS
    copies = []
    for i in range(PARTS):
        block = pl.ds(i * part, part)
        copies.append(pltpu.make_async_copy(x_ref.at[block], in_ref.at[block], x_sem.at[i]))
        copies[-1].start()
    tables = []
    for i in range(count):
        tables.append(pltpu.make_async_copy(refs[i], refs[count + 1 + i], t_sem.at[i]))
        tables[-1].start()
    for i in range(cores * slabs):
        if i * 128 % part == 0:
            copies[i * 128 // part].wait()
        o_ref[:, i // slabs, i % slabs] = columns_first(in_ref[i * 128 : (i + 1) * 128, :], pairs)
    for copy in tables:
        copy.wait()


def last_kernel(x_ref, o_ref, out_ref, sem):
    _, cores, slabs, _, _ = x_ref.shape
    copies = []
    for i in range(cores * slabs):
        block = pl.ds(i * 128, 128)
        out_ref[i * 128 : (i + 1) * 128, :] = rows_first(x_ref[:, i // slabs, i % slabs])
        copies.append(pltpu.make_async_copy(out_ref.at[block], o_ref.at[block], sem.at[i]))
        copies[-1].start()
    for copy in copies:
        copy.wait()


def placed(lines, offset, ext_refs, cells, lanes_per_block):
    lanes = lines[0].shape[1]
    circle = lanes // lanes_per_block * cells
    wrapped = offset & (circle - 1)
    step = (wrapped >> (cells.bit_length() - 1)) * lanes_per_block
    before = (step + lanes_per_block) & (lanes - 1)
    after = (step + lanes - lanes_per_block) & (lanes - 1)
    for line, ext_ref in zip(lines, ext_refs):
        ext_ref[0:cells] = pltpu.roll(line, before, 1)
        ext_ref[cells : 2 * cells] = pltpu.roll(line, step, 1)
        ext_ref[2 * cells : 2 * cells + 8] = pltpu.roll(line[0:8], after, 1)
    return cells - 1 - (wrapped & (cells - 1))


def tapped(start, weights, ext_refs, cells):
    totals = []
    for ext_ref in ext_refs:
        total = None
        for k in range(4):
            term = weights[k] * ext_ref[pl.ds(start + k, cells), :]
            total = term if total is None else total + term
        totals.append(total)
    return totals


def here(levels):
    lon = lax.axis_index("lon")
    return lax.div(lon * levels, lax.axis_size("lon")), lax.rem(lon, 2)


def first_pass(x_ref, slab, row, level, off_ref, w_ref, o_ref, turn_ref, ext_ref, cells):
    per_set = turn_ref.shape[2] // x_ref.shape[0]
    sets = x_ref.shape[2] // per_set
    for g in range(sets):
        turn_ref[g] = rows_first(x_ref[:, slab, g * per_set : (g + 1) * per_set])
    count = 128 // cells
    exts = [[ext_ref[i].at[g] for g in range(sets)] for i in range(count)]
    starts = []
    for i in range(count):
        lines = [turn_ref[g, i * cells : (i + 1) * cells, :] for g in range(sets)]
        starts.append(placed(lines, off_ref[level, row + i], exts[i], cells, per_set))
    for i in range(count):
        values = tapped(starts[i], [w_ref[k, level, row + i] for k in range(4)], exts[i], cells)
        for g in range(sets):
            o_ref[g * 128 + i * cells : g * 128 + (i + 1) * cells, :] = values[g]


def rows_done(slab, half, window_ref, first_place, level, core, tables, o_ref, turn_ref, ext_ref, cells, use=1):
    off_ref, w_ref, toff_ref, tw_ref = tables
    groups = o_ref.shape[0]
    per_set = turn_ref.shape[2] // groups
    sets = o_ref.shape[2] // per_set
    rows = 2 * half
    per_slab = 128 // cells
    first_row = lax.axis_index("band") * rows
    last_row = lax.axis_size("band") * rows - 1
    half_row = core * half
    first = half_row + slab * per_slab
    exts = [[ext_ref[use * per_slab + i].at[g] for g in range(sets)] for i in range(per_slab)]
    starts = []
    for i in range(per_slab):
        row = first + i
        shift = toff_ref[level, row]
        totals = [None] * sets
        for k in range(4):
            source = jnp.clip(first_row + row + (k - 1) - shift, 0, last_row) - first_row - half_row - first_place
            weight = tw_ref[k, level, row]
            where = pl.ds(pl.multiple_of(source * cells, cells), cells)
            for g in range(sets):
                term = weight * window_ref[g, where, :]
                totals[g] = term if totals[g] is None else totals[g] + term
        starts.append(placed(totals, off_ref[level, row], exts[i], cells, per_set))
    for i in range(per_slab):
        values = tapped(starts[i], [w_ref[k, level, first + i] for k in range(4)], exts[i], cells)
        for g in range(sets):
            turn_ref[g, i * cells : (i + 1) * cells, :] = values[g]
    for g in range(sets):
        o_ref[:, slab, g * per_set : (g + 1) * per_set] = columns_first(turn_ref[g], groups)


def edge_kernel(cells, levels, half, far, x_ref, off_ref, w_ref, o_ref, turn_ref, ext_ref):
    level, core = here(levels)
    slab = (core if far else 1 - core) * (x_ref.shape[1] - 1)
    row = core * half + slab * (128 // cells)
    first_pass(x_ref, slab, row, level, off_ref, w_ref, o_ref, turn_ref, ext_ref, cells)


def inner_kernel(
    cells, levels, half, x_ref, far_ref, near_ref, halo_ref, off_ref, w_ref, toff_ref, tw_ref, o_ref, mid_ref, own_ref, turn_ref, ext_ref
):
    level, core = here(levels)
    sets = turn_ref.shape[0]
    row = core * half + 128 // cells
    first_pass(x_ref, 1, row, level, off_ref, w_ref, mid_ref, turn_ref, ext_ref, cells)
    for g in range(sets):
        part = slice(g * 128, (g + 1) * 128)
        own_ref[g, pl.ds(pl.multiple_of(128 + core * 256, 128), 128), :] = far_ref[part, :]
        own_ref[g, 256:384, :] = mid_ref[part, :]
        own_ref[g, pl.ds(pl.multiple_of(384 - core * 256, 128), 128), :] = near_ref[part, :]
        own_ref[g, pl.ds(pl.multiple_of(512 - core * 512, 128), 128), :] = halo_ref[1 - core, part, :]
    tables = (off_ref, w_ref, toff_ref, tw_ref)
    for use, slab in ((1, 1), (2, 2 - 2 * core)):
        rows_done(slab, half, own_ref, -(128 // cells), level, core, tables, o_ref, turn_ref, ext_ref, cells, use)


def outer_kernel(
    cells, levels, half, edge_ref, mid_ref, halo_ref, off_ref, w_ref, toff_ref, tw_ref, i_ref, o_ref, own_ref, turn_ref, ext_ref
):
    level, core = here(levels)
    for g in range(turn_ref.shape[0]):
        part = slice(g * 128, (g + 1) * 128)
        own_ref[g, pl.ds(pl.multiple_of(core * 256, 128), 128), :] = halo_ref[part, :]
        own_ref[g, 128:256, :] = edge_ref[part, :]
        own_ref[g, pl.ds(pl.multiple_of((1 - core) * 256, 128), 128), :] = mid_ref[part, :]
    slab = core * 2
    first_place = (slab - 1) * (128 // cells)
    tables = (off_ref, w_ref, toff_ref, tw_ref)
    rows_done(slab, half, own_ref, first_place, level, core, tables, o_ref, turn_ref, ext_ref, cells)


def exchanged(x):
    return lax.all_to_all(x, "lon", 0, 0, tiled=True)


def per_device(tracers, lon_offset, lon_weights, lat_offset, lat_weights):
    rows, cells, columns = tracers.shape
    levels = lon_offset.shape[1]
    groups = lax.axis_size("lon")
    bands = lax.axis_size("band")
    flat = rows * cells
    half = rows // 2
    slabs = half * cells // 128
    per_set = 128 // groups
    sets = columns * 2 // groups // per_set
    f32 = jnp.float32
    vspec = pl.BlockSpec(memory_space=VMEM)
    sspec = pl.BlockSpec(memory_space=SMEM)
    hspec = pl.BlockSpec(memory_space=pltpu.HBM)
    tables = (lon_offset.T, lon_weights.transpose(0, 2, 1), lat_offset.T, lat_weights.transpose(0, 2, 1))
    assert slabs == 3 and REACH * cells == 128 and columns == 128
    sent = jax.ShapeDtypeStruct((groups // 2, 2, slabs, sets * per_set, 128), f32)
    slab_lines = jax.ShapeDtypeStruct((sets * 128, 128), f32)
    gathered_shape = (groups, *sent.shape[2:])
    turn = VMEM((sets, 128, 128), f32)
    ext = (VMEM((sets, 2 * cells + 8, 128), f32),) * (3 * 128 // cells)
    own = VMEM((sets, 3 * 128, 128), f32)

    def call(kernel, out_shape, in_specs, scratch, *args, aliases={}):
        return pl.pallas_call(
            kernel,
            out_shape=out_shape,
            in_specs=in_specs,
            out_specs=jax.tree.map(lambda x: vspec if isinstance(x, jax.ShapeDtypeStruct) else sspec, out_shape),
            scratch_shapes=scratch,
            input_output_aliases=aliases,
            compiler_params=PARAMS,
        )(*args)

    given = [pltpu.with_memory_space_constraint(x, pltpu.HBM) for x in (tracers.reshape(flat, columns), *tables)]
    spread, *tables = call(
        split_kernel,
        [sent] + [SMEM(x.shape, x.dtype) for x in tables],
        [hspec] * 5,
        [VMEM((flat, columns), f32), DMA((PARTS,)), DMA((4,))],
        *given,
    )
    tables = [pltpu.with_memory_space_constraint(x, SMEM) for x in tables]
    gathered = exchanged(spread.reshape(gathered_shape))

    def edge(far):
        kernel = functools.partial(edge_kernel, cells, levels, half, far)
        return call(kernel, slab_lines, [vspec, sspec, sspec], [turn, ext], gathered, *tables[:2])

    far = edge(True)
    pairs = []
    for n in range(bands - 1):
        for lon in range(1, groups, 2):
            lower, upper = n * groups + lon, (n + 1) * groups + lon - 1
            pairs += [(lower, upper), (upper, lower)]
    far_halo = lax.ppermute(far, ("band", "lon"), pairs)
    near = edge(False)
    near_halo = lax.all_gather(near, "lon", axis_index_groups=[[lon, lon + 1] for lon in range(0, groups, 2)])
    out, mid = call(
        functools.partial(inner_kernel, cells, levels, half),
        [jax.ShapeDtypeStruct(gathered_shape, f32), slab_lines],
        [vspec] * 4 + [sspec] * 4,
        [VMEM((sets, 5 * 128, 128), f32), turn, ext],
        gathered,
        far,
        near,
        near_halo,
        *tables,
    )
    out = call(
        functools.partial(outer_kernel, cells, levels, half),
        jax.ShapeDtypeStruct(gathered_shape, f32),
        [vspec] * 3 + [sspec] * 4 + [vspec],
        [own, turn, ext],
        far,
        mid,
        far_halo,
        *tables,
        out,
        aliases={7: 0},
    )
    last = pl.pallas_call(
        last_kernel,
        out_shape=jax.ShapeDtypeStruct((flat, columns), f32),
        in_specs=[vspec],
        out_specs=hspec,
        scratch_shapes=[VMEM((flat, columns), f32), DMA((flat // 128,))],
        compiler_params=PARAMS,
        name="last",
    )(exchanged(out).reshape(sent.shape))
    return last.reshape(rows, cells, columns)


def solution(mesh):
    return jax.shard_map(
        per_device,
        mesh=mesh,
        in_specs=(
            P("band", "lon", None),
            P("band", None),
            P(None, "band", None),
            P("band", None),
            P(None, "band", None),
        ),
        out_specs=P("band", "lon", None),
        check_vma=False,
    )
```

```python
import functools

import jax
import jax.numpy as jnp
from jax import lax
from jax.experimental import pallas as pl
from jax.experimental.pallas import tpu as pltpu
from jax.sharding import PartitionSpec as P


REACH = 8
PARTS = 1
VMEM = pltpu.VMEM
SMEM = pltpu.SMEM
DMA = pltpu.SemaphoreType.DMA
PARAMS = pltpu.CompilerParams(vmem_limit_bytes=8 * 1024 * 1024)


def columns_first(block, groups):
    return block.T.reshape(groups, block.shape[1] // groups, block.shape[0])


def rows_first(slab):
    return slab.reshape(slab.shape[0] * slab.shape[1], slab.shape[2]).T


def split_kernel(x_ref, *refs):
    count = (len(refs) - 4) // 2
    o_ref = refs[count]
    in_ref, x_sem, t_sem = refs[-3:]
    pairs, cores, slabs, _, _ = o_ref.shape
    part = x_ref.shape[0] // PARTS
    copies = []
    for i in range(PARTS):
        block = pl.ds(i * part, part)
        copies.append(pltpu.make_async_copy(x_ref.at[block], in_ref.at[block], x_sem.at[i]))
        copies[-1].start()
    tables = []
    for i in range(count):
        tables.append(pltpu.make_async_copy(refs[i], refs[count + 1 + i], t_sem.at[i]))
        tables[-1].start()
    for i in range(cores * slabs):
        if i * 128 % part == 0:
            copies[i * 128 // part].wait()
        o_ref[:, i // slabs, i % slabs] = columns_first(in_ref[i * 128 : (i + 1) * 128, :], pairs)
    for copy in tables:
        copy.wait()


def last_kernel(x_ref, o_ref, out_ref, sem):
    _, cores, slabs, _, _ = x_ref.shape
    copies = []
    for i in range(cores * slabs):
        block = pl.ds(i * 128, 128)
        out_ref[i * 128 : (i + 1) * 128, :] = rows_first(x_ref[:, i // slabs, i % slabs])
        copies.append(pltpu.make_async_copy(out_ref.at[block], o_ref.at[block], sem.at[i]))
        copies[-1].start()
    for copy in copies:
        copy.wait()


def placed(lines, offset, ext_refs, cells, lanes_per_block):
    lanes = lines[0].shape[1]
    circle = lanes // lanes_per_block * cells
    wrapped = offset & (circle - 1)
    step = (wrapped >> (cells.bit_length() - 1)) * lanes_per_block
    before = (step + lanes_per_block) & (lanes - 1)
    after = (step + lanes - lanes_per_block) & (lanes - 1)
    for line, ext_ref in zip(lines, ext_refs):
        ext_ref[0:cells] = pltpu.roll(line, before, 1)
        ext_ref[cells : 2 * cells] = pltpu.roll(line, step, 1)
        ext_ref[2 * cells : 2 * cells + 8] = pltpu.roll(line[0:8], after, 1)
    return cells - 1 - (wrapped & (cells - 1))


def tapped(start, weights, ext_refs, cells):
    totals = []
    for ext_ref in ext_refs:
        total = None
        for k in range(4):
            term = weights[k] * ext_ref[pl.ds(start + k, cells), :]
            total = term if total is None else total + term
        totals.append(total)
    return totals


def here(levels):
    lon = lax.axis_index("lon")
    return lax.div(lon * levels, lax.axis_size("lon")), lax.rem(lon, 2)


def first_pass(x_ref, slab, row, level, off_ref, w_ref, o_ref, turn_ref, ext_ref, cells):
    per_set = turn_ref.shape[2] // x_ref.shape[0]
    sets = x_ref.shape[2] // per_set
    for g in range(sets):
        turn_ref[g] = rows_first(x_ref[:, slab, g * per_set : (g + 1) * per_set])
    count = 128 // cells
    exts = [[ext_ref[i].at[g] for g in range(sets)] for i in range(count)]
    starts = []
    for i in range(count):
        lines = [turn_ref[g, i * cells : (i + 1) * cells, :] for g in range(sets)]
        starts.append(placed(lines, off_ref[level, row + i], exts[i], cells, per_set))
    for i in range(count):
        values = tapped(starts[i], [w_ref[k, level, row + i] for k in range(4)], exts[i], cells)
        for g in range(sets):
            o_ref[g * 128 + i * cells : g * 128 + (i + 1) * cells, :] = values[g]


def rows_done(slab, half, window_ref, base, level, core, tables, o_ref, turn_ref, ext_ref, cells, use=1):
    off_ref, w_ref, toff_ref, tw_ref = tables
    groups = o_ref.shape[0]
    per_set = turn_ref.shape[2] // groups
    sets = o_ref.shape[2] // per_set
    rows = 2 * half
    per_slab = 128 // cells
    first = core * half + slab * per_slab
    origin = (lax.axis_index("band") * rows + first - base) * cells
    end = (lax.axis_size("band") * rows - 1) * cells - origin
    exts = [[ext_ref[use * per_slab + i].at[g] for g in range(sets)] for i in range(per_slab)]
    starts = []
    for i in range(per_slab):
        row = first + i
        shift = toff_ref[level, row] * cells
        totals = [None] * sets
        for k in range(4):
            source = jnp.minimum(jnp.maximum((base + i + k - 1) * cells - shift, -origin), end)
            weight = tw_ref[k, level, row]
            where = pl.ds(pl.multiple_of(source, cells), cells)
            for g in range(sets):
                term = weight * window_ref[g, where, :]
                totals[g] = term if totals[g] is None else totals[g] + term
        starts.append(placed(totals, off_ref[level, row], exts[i], cells, per_set))
    for i in range(per_slab):
        values = tapped(starts[i], [w_ref[k, level, first + i] for k in range(4)], exts[i], cells)
        for g in range(sets):
            turn_ref[g, i * cells : (i + 1) * cells, :] = values[g]
    for g in range(sets):
        o_ref[:, slab, g * per_set : (g + 1) * per_set] = columns_first(turn_ref[g], groups)


def edge_kernel(cells, levels, half, far, x_ref, off_ref, w_ref, o_ref, turn_ref, ext_ref):
    level, core = here(levels)
    slab = (core if far else 1 - core) * (x_ref.shape[1] - 1)
    row = core * half + slab * (128 // cells)
    first_pass(x_ref, slab, row, level, off_ref, w_ref, o_ref, turn_ref, ext_ref, cells)


def inner_kernel(
    cells, levels, half, x_ref, far_ref, near_ref, halo_ref, off_ref, w_ref, toff_ref, tw_ref, o_ref, mid_ref, own_ref, turn_ref, ext_ref
):
    level, core = here(levels)
    sets = turn_ref.shape[0]
    row = core * half + 128 // cells
    first_pass(x_ref, 1, row, level, off_ref, w_ref, mid_ref, turn_ref, ext_ref, cells)
    for g in range(sets):
        part = slice(g * 128, (g + 1) * 128)
        own_ref[g, pl.ds(pl.multiple_of(128 + core * 256, 128), 128), :] = far_ref[part, :]
        own_ref[g, 256:384, :] = mid_ref[part, :]
        own_ref[g, pl.ds(pl.multiple_of(384 - core * 256, 128), 128), :] = near_ref[part, :]
        own_ref[g, pl.ds(pl.multiple_of(512 - core * 512, 128), 128), :] = halo_ref[1 - core, part, :]
    tables = (off_ref, w_ref, toff_ref, tw_ref)
    for use, slab in ((1, 1), (2, 2 - 2 * core)):
        rows_done(slab, half, own_ref, (slab + 1) * (128 // cells), level, core, tables, o_ref, turn_ref, ext_ref, cells, use)


def outer_kernel(
    cells, levels, half, edge_ref, mid_ref, halo_ref, off_ref, w_ref, toff_ref, tw_ref, i_ref, o_ref, own_ref, turn_ref, ext_ref
):
    level, core = here(levels)
    for g in range(turn_ref.shape[0]):
        part = slice(g * 128, (g + 1) * 128)
        own_ref[g, pl.ds(pl.multiple_of(core * 256, 128), 128), :] = halo_ref[part, :]
        own_ref[g, 128:256, :] = edge_ref[part, :]
        own_ref[g, pl.ds(pl.multiple_of((1 - core) * 256, 128), 128), :] = mid_ref[part, :]
    slab = core * 2
    tables = (off_ref, w_ref, toff_ref, tw_ref)
    rows_done(slab, half, own_ref, 128 // cells, level, core, tables, o_ref, turn_ref, ext_ref, cells)


def exchanged(x):
    return lax.all_to_all(x, "lon", 0, 0, tiled=True)


def per_device(tracers, lon_offset, lon_weights, lat_offset, lat_weights):
    rows, cells, columns = tracers.shape
    levels = lon_offset.shape[1]
    groups = lax.axis_size("lon")
    bands = lax.axis_size("band")
    flat = rows * cells
    half = rows // 2
    slabs = half * cells // 128
    per_set = 128 // groups
    sets = columns * 2 // groups // per_set
    f32 = jnp.float32
    vspec = pl.BlockSpec(memory_space=VMEM)
    sspec = pl.BlockSpec(memory_space=SMEM)
    hspec = pl.BlockSpec(memory_space=pltpu.HBM)
    tables = (lon_offset.T, lon_weights.transpose(0, 2, 1), lat_offset.T, lat_weights.transpose(0, 2, 1))
    assert slabs == 3 and REACH * cells == 128 and columns == 128
    sent = jax.ShapeDtypeStruct((groups // 2, 2, slabs, sets * per_set, 128), f32)
    slab_lines = jax.ShapeDtypeStruct((sets * 128, 128), f32)
    gathered_shape = (groups, *sent.shape[2:])
    turn = VMEM((sets, 128, 128), f32)
    ext = (VMEM((sets, 2 * cells + 8, 128), f32),) * (3 * 128 // cells)
    own = VMEM((sets, 3 * 128, 128), f32)

    def call(kernel, out_shape, in_specs, scratch, *args, aliases={}):
        return pl.pallas_call(
            kernel,
            out_shape=out_shape,
            in_specs=in_specs,
            out_specs=jax.tree.map(lambda x: vspec if isinstance(x, jax.ShapeDtypeStruct) else sspec, out_shape),
            scratch_shapes=scratch,
            input_output_aliases=aliases,
            compiler_params=PARAMS,
        )(*args)

    given = [pltpu.with_memory_space_constraint(x, pltpu.HBM) for x in (tracers.reshape(flat, columns), *tables)]
    spread, *tables = call(
        split_kernel,
        [sent] + [SMEM(x.shape, x.dtype) for x in tables],
        [hspec] * 5,
        [VMEM((flat, columns), f32), DMA((PARTS,)), DMA((4,))],
        *given,
    )
    tables = [pltpu.with_memory_space_constraint(x, SMEM) for x in tables]
    gathered = exchanged(spread.reshape(gathered_shape))

    def edge(far):
        kernel = functools.partial(edge_kernel, cells, levels, half, far)
        return call(kernel, slab_lines, [vspec, sspec, sspec], [turn, ext], gathered, *tables[:2])

    far = edge(True)
    pairs = []
    for n in range(bands - 1):
        for lon in range(1, groups, 2):
            lower, upper = n * groups + lon, (n + 1) * groups + lon - 1
            pairs += [(lower, upper), (upper, lower)]
    far_halo = lax.ppermute(far, ("band", "lon"), pairs)
    near = edge(False)
    near_halo = lax.all_gather(near, "lon", axis_index_groups=[[lon, lon + 1] for lon in range(0, groups, 2)])
    out, mid = call(
        functools.partial(inner_kernel, cells, levels, half),
        [jax.ShapeDtypeStruct(gathered_shape, f32), slab_lines],
        [vspec] * 4 + [sspec] * 4,
        [VMEM((sets, 5 * 128, 128), f32), turn, ext],
        gathered,
        far,
        near,
        near_halo,
        *tables,
    )
    out = call(
        functools.partial(outer_kernel, cells, levels, half),
        jax.ShapeDtypeStruct(gathered_shape, f32),
        [vspec] * 3 + [sspec] * 4 + [vspec],
        [own, turn, ext],
        far,
        mid,
        far_halo,
        *tables,
        out,
        aliases={7: 0},
    )
    last = pl.pallas_call(
        last_kernel,
        out_shape=jax.ShapeDtypeStruct((flat, columns), f32),
        in_specs=[vspec],
        out_specs=hspec,
        scratch_shapes=[VMEM((flat, columns), f32), DMA((flat // 128,))],
        compiler_params=PARAMS,
        name="last",
    )(exchanged(out).reshape(sent.shape))
    return last.reshape(rows, cells, columns)


def solution(mesh):
    return jax.shard_map(
        per_device,
        mesh=mesh,
        in_specs=(
            P("band", "lon", None),
            P("band", None),
            P(None, "band", None),
            P("band", None),
            P(None, "band", None),
        ),
        out_specs=P("band", "lon", None),
        check_vma=False,
    )
```

```python
import functools

import jax
import jax.numpy as jnp
from jax import lax
from jax.experimental import pallas as pl
from jax.experimental.pallas import tpu as pltpu
from jax.sharding import PartitionSpec as P


REACH = 8
PARTS = 1
VMEM = pltpu.VMEM
SMEM = pltpu.SMEM
DMA = pltpu.SemaphoreType.DMA
PARAMS = pltpu.CompilerParams(vmem_limit_bytes=8 * 1024 * 1024)


def columns_first(block, groups):
    return block.T.reshape(groups, block.shape[1] // groups, block.shape[0])


def rows_first(slab):
    return slab.reshape(slab.shape[0] * slab.shape[1], slab.shape[2]).T


def split_kernel(x_ref, *refs):
    count = (len(refs) - 4) // 2
    o_ref = refs[count]
    in_ref, x_sem, t_sem = refs[-3:]
    pairs, cores, slabs, _, _ = o_ref.shape
    part = x_ref.shape[0] // PARTS
    copies = []
    for i in range(PARTS):
        block = pl.ds(i * part, part)
        copies.append(pltpu.make_async_copy(x_ref.at[block], in_ref.at[block], x_sem.at[i]))
        copies[-1].start()
    tables = []
    for i in range(count):
        tables.append(pltpu.make_async_copy(refs[i], refs[count + 1 + i], t_sem.at[i]))
        tables[-1].start()
    for i in range(cores * slabs):
        if i * 128 % part == 0:
            copies[i * 128 // part].wait()
        o_ref[:, i // slabs, i % slabs] = columns_first(in_ref[i * 128 : (i + 1) * 128, :], pairs)
    for copy in tables:
        copy.wait()


def last_kernel(x_ref, o_ref, out_ref, sem):
    _, cores, slabs, _, _ = x_ref.shape
    copies = []
    for i in range(cores * slabs):
        block = pl.ds(i * 128, 128)
        out_ref[i * 128 : (i + 1) * 128, :] = rows_first(x_ref[:, i // slabs, i % slabs])
        copies.append(pltpu.make_async_copy(out_ref.at[block], o_ref.at[block], sem.at[i]))
        copies[-1].start()
    for copy in copies:
        copy.wait()


def placed(lines, offset, ext_refs, cells, lanes_per_block):
    lanes = lines[0].shape[1]
    step = (offset >> (cells // lanes_per_block).bit_length() - 1) & (lanes - lanes_per_block)
    before = (step + lanes_per_block) & (lanes - 1)
    after = (step + lanes - lanes_per_block) & (lanes - 1)
    for line, ext_ref in zip(lines, ext_refs):
        ext_ref[0:cells] = pltpu.roll(line, before, 1)
        ext_ref[cells : 2 * cells] = pltpu.roll(line, step, 1)
        ext_ref[2 * cells : 2 * cells + 8] = pltpu.roll(line[0:8], after, 1)
    return cells - 1 - (offset & (cells - 1))


def tapped(start, weights, ext_refs, cells):
    totals = []
    for ext_ref in ext_refs:
        total = None
        for k in range(4):
            term = weights[k] * ext_ref[pl.ds(start + k, cells), :]
            total = term if total is None else total + term
        totals.append(total)
    return totals


def here(levels):
    lon = lax.axis_index("lon")
    return lax.div(lon * levels, lax.axis_size("lon")), lax.rem(lon, 2)


def first_pass(x_ref, slab, row, level, off_ref, w_ref, o_ref, turn_ref, ext_ref, cells):
    per_set = turn_ref.shape[2] // x_ref.shape[0]
    sets = x_ref.shape[2] // per_set
    for g in range(sets):
        turn_ref[g] = rows_first(x_ref[:, slab, g * per_set : (g + 1) * per_set])
    count = 128 // cells
    exts = [[ext_ref[i].at[g] for g in range(sets)] for i in range(count)]
    starts = []
    for i in range(count):
        lines = [turn_ref[g, i * cells : (i + 1) * cells, :] for g in range(sets)]
        starts.append(placed(lines, off_ref[level, row + i], exts[i], cells, per_set))
    for i in range(count):
        values = tapped(starts[i], [w_ref[k, level, row + i] for k in range(4)], exts[i], cells)
        for g in range(sets):
            o_ref[g * 128 + i * cells : g * 128 + (i + 1) * cells, :] = values[g]


def rows_done(slab, half, window_ref, base, level, core, tables, o_ref, turn_ref, ext_ref, cells, use=1):
    off_ref, w_ref, toff_ref, tw_ref = tables
    groups = o_ref.shape[0]
    per_set = turn_ref.shape[2] // groups
    sets = o_ref.shape[2] // per_set
    rows = 2 * half
    per_slab = 128 // cells
    first = core * half + slab * per_slab
    origin = (lax.axis_index("band") * rows + first - base) * cells
    end = (lax.axis_size("band") * rows - 1) * cells - origin
    exts = [[ext_ref[use * per_slab + i].at[g] for g in range(sets)] for i in range(per_slab)]
    starts = []
    for i in range(per_slab):
        row = first + i
        shift = toff_ref[level, row] * cells
        totals = [None] * sets
        for k in range(4):
            source = jnp.minimum(jnp.maximum((base + i + k - 1) * cells - shift, -origin), end)
            weight = tw_ref[k, level, row]
            where = pl.ds(pl.multiple_of(source, cells), cells)
            for g in range(sets):
                term = weight * window_ref[g, where, :]
                totals[g] = term if totals[g] is None else totals[g] + term
        starts.append(placed(totals, off_ref[level, row], exts[i], cells, per_set))
    for i in range(per_slab):
        values = tapped(starts[i], [w_ref[k, level, first + i] for k in range(4)], exts[i], cells)
        for g in range(sets):
            turn_ref[g, i * cells : (i + 1) * cells, :] = values[g]
    for g in range(sets):
        o_ref[:, slab, g * per_set : (g + 1) * per_set] = columns_first(turn_ref[g], groups)


def edge_kernel(cells, levels, half, far, x_ref, off_ref, w_ref, o_ref, turn_ref, ext_ref):
    level, core = here(levels)
    slab = (core if far else 1 - core) * (x_ref.shape[1] - 1)
    row = core * half + slab * (128 // cells)
    first_pass(x_ref, slab, row, level, off_ref, w_ref, o_ref, turn_ref, ext_ref, cells)


def inner_kernel(
    cells, levels, half, x_ref, far_ref, near_ref, halo_ref, off_ref, w_ref, toff_ref, tw_ref, o_ref, mid_ref, own_ref, turn_ref, ext_ref
):
    level, core = here(levels)
    sets = turn_ref.shape[0]
    row = core * half + 128 // cells
    first_pass(x_ref, 1, row, level, off_ref, w_ref, mid_ref, turn_ref, ext_ref, cells)
    for g in range(sets):
        part = slice(g * 128, (g + 1) * 128)
        own_ref[g, pl.ds(pl.multiple_of(128 + core * 256, 128), 128), :] = far_ref[part, :]
        own_ref[g, 256:384, :] = mid_ref[part, :]
        own_ref[g, pl.ds(pl.multiple_of(384 - core * 256, 128), 128), :] = near_ref[part, :]
        own_ref[g, pl.ds(pl.multiple_of(512 - core * 512, 128), 128), :] = halo_ref[1 - core, part, :]
    tables = (off_ref, w_ref, toff_ref, tw_ref)
    for use, slab in ((1, 1), (2, 2 - 2 * core)):
        rows_done(slab, half, own_ref, (slab + 1) * (128 // cells), level, core, tables, o_ref, turn_ref, ext_ref, cells, use)


def outer_kernel(
    cells, levels, half, edge_ref, mid_ref, halo_ref, off_ref, w_ref, toff_ref, tw_ref, i_ref, o_ref, own_ref, turn_ref, ext_ref
):
    level, core = here(levels)
    for g in range(turn_ref.shape[0]):
        part = slice(g * 128, (g + 1) * 128)
        own_ref[g, pl.ds(pl.multiple_of(core * 256, 128), 128), :] = halo_ref[part, :]
        own_ref[g, 128:256, :] = edge_ref[part, :]
        own_ref[g, pl.ds(pl.multiple_of((1 - core) * 256, 128), 128), :] = mid_ref[part, :]
    slab = core * 2
    tables = (off_ref, w_ref, toff_ref, tw_ref)
    rows_done(slab, half, own_ref, 128 // cells, level, core, tables, o_ref, turn_ref, ext_ref, cells)


def exchanged(x):
    return lax.all_to_all(x, "lon", 0, 0, tiled=True)


def per_device(tracers, lon_offset, lon_weights, lat_offset, lat_weights):
    rows, cells, columns = tracers.shape
    levels = lon_offset.shape[1]
    groups = lax.axis_size("lon")
    bands = lax.axis_size("band")
    flat = rows * cells
    half = rows // 2
    slabs = half * cells // 128
    per_set = 128 // groups
    sets = columns * 2 // groups // per_set
    f32 = jnp.float32
    vspec = pl.BlockSpec(memory_space=VMEM)
    sspec = pl.BlockSpec(memory_space=SMEM)
    hspec = pl.BlockSpec(memory_space=pltpu.HBM)
    tables = (lon_offset.T, lon_weights.transpose(0, 2, 1), lat_offset.T, lat_weights.transpose(0, 2, 1))
    assert slabs == 3 and REACH * cells == 128 and columns == 128
    sent = jax.ShapeDtypeStruct((groups // 2, 2, slabs, sets * per_set, 128), f32)
    slab_lines = jax.ShapeDtypeStruct((sets * 128, 128), f32)
    gathered_shape = (groups, *sent.shape[2:])
    turn = VMEM((sets, 128, 128), f32)
    ext = (VMEM((sets, 2 * cells + 8, 128), f32),) * (3 * 128 // cells)
    own = VMEM((sets, 3 * 128, 128), f32)

    def call(kernel, out_shape, in_specs, scratch, *args, aliases={}):
        return pl.pallas_call(
            kernel,
            out_shape=out_shape,
            in_specs=in_specs,
            out_specs=jax.tree.map(lambda x: vspec if isinstance(x, jax.ShapeDtypeStruct) else sspec, out_shape),
            scratch_shapes=scratch,
            input_output_aliases=aliases,
            compiler_params=PARAMS,
        )(*args)

    given = [pltpu.with_memory_space_constraint(x, pltpu.HBM) for x in (tracers.reshape(flat, columns), *tables)]
    spread, *tables = call(
        split_kernel,
        [sent] + [SMEM(x.shape, x.dtype) for x in tables],
        [hspec] * 5,
        [VMEM((flat, columns), f32), DMA((PARTS,)), DMA((4,))],
        *given,
    )
    tables = [pltpu.with_memory_space_constraint(x, SMEM) for x in tables]
    gathered = exchanged(spread.reshape(gathered_shape))

    def edge(far):
        kernel = functools.partial(edge_kernel, cells, levels, half, far)
        return call(kernel, slab_lines, [vspec, sspec, sspec], [turn, ext], gathered, *tables[:2])

    far = edge(True)
    pairs = []
    for n in range(bands - 1):
        for lon in range(1, groups, 2):
            lower, upper = n * groups + lon, (n + 1) * groups + lon - 1
            pairs += [(lower, upper), (upper, lower)]
    far_halo = lax.ppermute(far, ("band", "lon"), pairs)
    near = edge(False)
    near_halo = lax.all_gather(near, "lon", axis_index_groups=[[lon, lon + 1] for lon in range(0, groups, 2)])
    out, mid = call(
        functools.partial(inner_kernel, cells, levels, half),
        [jax.ShapeDtypeStruct(gathered_shape, f32), slab_lines],
        [vspec] * 4 + [sspec] * 4,
        [VMEM((sets, 5 * 128, 128), f32), turn, ext],
        gathered,
        far,
        near,
        near_halo,
        *tables,
    )
    out = call(
        functools.partial(outer_kernel, cells, levels, half),
        jax.ShapeDtypeStruct(gathered_shape, f32),
        [vspec] * 3 + [sspec] * 4 + [vspec],
        [own, turn, ext],
        far,
        mid,
        far_halo,
        *tables,
        out,
        aliases={7: 0},
    )
    last = pl.pallas_call(
        last_kernel,
        out_shape=jax.ShapeDtypeStruct((flat, columns), f32),
        in_specs=[vspec],
        out_specs=hspec,
        scratch_shapes=[VMEM((flat, columns), f32), DMA((flat // 128,))],
        compiler_params=PARAMS,
        name="last",
    )(exchanged(out).reshape(sent.shape))
    return last.reshape(rows, cells, columns)


def solution(mesh):
    return jax.shard_map(
        per_device,
        mesh=mesh,
        in_specs=(
            P("band", "lon", None),
            P("band", None),
            P(None, "band", None),
            P("band", None),
            P(None, "band", None),
        ),
        out_specs=P("band", "lon", None),
        check_vma=False,
    )
```
